32 devices in a mesh: gx: 4 (over x, core), gy: 4 (over z), gz: 2 (over y).
Axes of the slice: x: 2, y: 2, z: 4, core: 2. Of those that a mesh axis runs over, the one named last changes fastest.
Arguments:
- right_side: float32 [3, 64, 64, 256], P(None, 'gx', 'gy', 'gz'), may hold values from -24 to 24
- labels: int32 [64, 64, 256], P('gx', 'gy', 'gz'), may hold values from 0 to 15
- colors: int32 [3, 64, 64, 256], P(None, 'gx', 'gy', 'gz'), may hold values from 0 to 3
- table: float32 [16], replicated, may hold values from 0.5 to 4
Outputs:
- preconditioned: float32 [3, 64, 64, 256], P(None, 'gx', 'gy', 'gz')
The draws below stay inside these ranges and needn't reach their ends.
All inputs are finite; a program needn't handle non-finite values.
Results may differ from the reference program's by a relative error of at most 0.00002.
Values sent between devices are 32-bit elements; how exact they have to be, the bound alone decides.
No kernel may reach another device: no remote copies, remote signals or barrier semaphores. Data moves between devices by JAX's collectives and lax.ppermute only.
A program may use at most 64 MiB of HBM per device.

```python
import math
import jax
import jax.numpy as jnp
from jax import lax

NSWEEP = 2
NCOL = 4
NCHEB = 4
NREG = 16
NX = 64
NY = 64
NZ = 256


def touch_ends(values, own_key, smallest, high):
    longest = values.shape.index(max(values.shape))
    spots = []
    for shift in (0, 1):
        where = [jax.random.randint(jax.random.fold_in(own_key, axis), (), 0, length) for axis, length in enumerate(values.shape)]
        where[longest] = (where[longest] + shift) % values.shape[longest]
        spots.append(tuple(where))
    return values.at[spots[0]].set(smallest).at[spots[1]].set(high)


def level_of(own_key, dims, cuts, least, top_value):
    def one(dim, shards_of):
        heights = jax.random.uniform(jax.random.fold_in(jax.random.fold_in(own_key, 6), dim), (shards_of,), jnp.float32, least / len(cuts), top_value / len(cuts))
        return jnp.repeat(jnp.exp(heights), dims[dim] // shards_of).reshape((-1,) + (1,) * (len(dims) - dim - 1))

    level = one(*cuts[0])
    for cut in cuts[1:]:
        level = level * one(*cut)
    return level


def scatter_about(stream_key, shape, scale, bound, cuts=(), dtype=jnp.bfloat16):
    values = scale * jax.random.normal(stream_key, shape, jnp.float32)
    if cuts:
        values = values * level_of(stream_key, shape, cuts, -0.22, 0.18)
    return jnp.clip(values, -bound, bound).astype(dtype)


def setup_inputs(seed: int = 0) -> dict:
    key_list = jax.random.split(jax.random.key(seed), 5)
    return {
        "right_side": scatter_about(key_list[0], (3, NX, NY, NZ), 4.0, 24.0, ((1, 4), (2, 4), (3, 2)), jnp.float32),
        "labels": touch_ends(jax.random.randint(key_list[1], (NX, NY, NZ), 0, NREG), jax.random.fold_in(key_list[1], 1), 0, NREG - 1).astype(jnp.int32),
        "colors": touch_ends(jax.random.randint(key_list[2], (3, NX, NY, NZ), 0, NCOL), jax.random.fold_in(key_list[2], 1), 0, NCOL - 1).astype(jnp.int32),
        "table": jnp.clip(jnp.exp(jax.random.uniform(key_list[3], (NREG,), jnp.float32, math.log(0.5), math.log(4.0))), 0.5, 4.0),
    }


def unit_step(direction):
    return tuple(1 if position == direction else 0 for position in range(3))


def lower_step(direction):
    return tuple(1 - element for element in unit_step(direction))


def upper_step(direction):
    return tuple(1 + element for element in unit_step(direction))


def window(values, corner_at, extent):
    leading = values.ndim - 3
    begin_at = (0,) * leading + tuple(corner_at)
    finish = tuple(values.shape[:leading]) + tuple(offset + length for offset, length in zip(corner_at, extent))
    return lax.slice(values, begin_at, finish)


def shrink(values, amount):
    return tuple(number - amount for number in values.shape[-3:])


def pad_cells(values):
    return jnp.pad(values, ((0, 0),) * (values.ndim - 3) + ((1, 1),) * 3)


def face_curl(padded):
    extent = shrink(padded, 1)
    anchor = (0, 0, 0)
    face_list = []
    for normal in range(3):
        second = (normal + 1) % 3
        third_axis = (normal + 2) % 3
        face_list.append(window(padded[second], anchor, extent) - window(padded[second], unit_step(third_axis), extent)
                         + window(padded[third_axis], unit_step(second), extent) - window(padded[third_axis], anchor, extent))
    return jnp.stack(face_list)


def curl_back(faces_in):
    extent = shrink(faces_in, 1)
    centre = (1, 1, 1)
    result = []
    for edge_axis in range(3):
        before = (edge_axis + 2) % 3
        next_axis = (edge_axis + 1) % 3
        result.append(window(faces_in[before], centre, extent) - window(faces_in[before], lower_step(next_axis), extent)
                      - window(faces_in[next_axis], centre, extent) + window(faces_in[next_axis], lower_step(before), extent))
    return jnp.stack(result)


def edge_apply(padded, conduct, keep_mask):
    faces_in = face_curl(padded) * keep_mask
    inner = window(padded, (1, 1, 1), shrink(padded, 2))
    return curl_back(faces_in) + conduct * inner


def node_apply(field_ext, cond_ext, mass_weight):
    wide_extent = shrink(field_ext, 1)
    narrow_extent = shrink(field_ext, 2)
    anchor = (0, 0, 0)
    coefficient = window(cond_ext, anchor, wide_extent)
    centre_values = window(field_ext, anchor, wide_extent)
    summed = mass_weight * window(cond_ext, (1, 1, 1), narrow_extent) * window(field_ext, (1, 1, 1), narrow_extent)
    for direction in range(3):
        edge_flux = coefficient * (window(field_ext, unit_step(direction), wide_extent) - centre_values)
        summed = summed + window(edge_flux, lower_step(direction), narrow_extent) - window(edge_flux, (1, 1, 1), narrow_extent)
    return summed


def nodal_rhs(padded):
    narrow_extent = shrink(padded, 2)
    centre = (1, 1, 1)
    pieces = []
    scalar_part = None
    for direction in range(3):
        own_values = window(padded[direction], centre, narrow_extent)
        below_values = window(padded[direction], lower_step(direction), narrow_extent)
        difference = below_values - own_values
        scalar_part = difference if direction == 0 else scalar_part + difference
        pieces.append(0.5 * (own_values + below_values))
    return jnp.stack([scalar_part] + pieces)


def chebyshev(rhs_fields, apply_fn, table):
    upper = 13.0 * jnp.max(table)
    lower = upper / 30.0
    centre_value = 0.5 * (upper + lower)
    half_width = 0.5 * (upper - lower)
    ratio = centre_value / half_width
    damping = 1.0 / ratio
    solved = jnp.zeros_like(rhs_fields)
    residue = rhs_fields
    step_dir = rhs_fields / centre_value
    for degree in range(NCHEB):
        solved = solved + step_dir
        if degree + 1 < NCHEB:
            residue = residue - apply_fn(step_dir)
            damping_next = 1.0 / (2.0 * ratio - damping)
            step_dir = damping_next * damping * step_dir + (2.0 * damping_next / half_width) * residue
            damping = damping_next
    return solved


def correction(field_ext):
    narrow_extent = shrink(field_ext, 2)
    centre = (1, 1, 1)
    pieces = []
    for direction in range(3):
        gradient = window(field_ext[0], upper_step(direction), narrow_extent) - window(field_ext[0], centre, narrow_extent)
        averaged = 0.5 * (window(field_ext[1 + direction], centre, narrow_extent) + window(field_ext[1 + direction], upper_step(direction), narrow_extent))
        pieces.append(gradient + averaged)
    return jnp.stack(pieces)


def reference(right_side, labels, colors, table):
    conduct = table[labels]
    diagonal = 16.0 + conduct
    extent_plus = tuple(number + 1 for number in labels.shape)
    keep_mask = jnp.ones(extent_plus, jnp.float32)
    for position in range(3):
        counter = lax.broadcasted_iota(jnp.int32, extent_plus, position)
        keep_mask = keep_mask * jnp.where(counter > 0, 1.0, 0.0).astype(jnp.float32)
    iterate = jnp.zeros_like(right_side)
    for sweep_index in range(NSWEEP):
        for colour in range(NCOL):
            residual = right_side - edge_apply(pad_cells(iterate), conduct, keep_mask)
            iterate = iterate + jnp.where(colors == colour, residual / diagonal, 0.0)
    cond_ext = pad_cells(conduct)
    rhs_fields = nodal_rhs(pad_cells(right_side))
    mass_weight = jnp.array([0.0, 1.0, 1.0, 1.0], jnp.float32).reshape(4, 1, 1, 1)

    def apply_nodal(fields):
        return node_apply(pad_cells(fields), cond_ext, mass_weight)

    solved = chebyshev(rhs_fields, apply_nodal, table)
    return iterate + correction(pad_cells(solved))
```

```python
import jax
import jax.numpy as jnp
from jax import lax
from jax.experimental import pallas as pl
from jax.experimental.pallas import tpu as pltpu
from jax.sharding import PartitionSpec as P

NSWEEP = 2
NCOL = 4
NCHEB = 4
HALO = NSWEEP * NCOL - 1
TILE = 8
LANES = 128
NFIELD = 7


def swap_pairs(count, parity):
    pairs = []
    for low in range(parity, count - 1, 2):
        pairs += [(low, low + 1), (low + 1, low)]
    return pairs


def swaps_of(count):
    return [swap_pairs(count, parity) for parity in (0, 1)]


def exchange(message, axis, pairs):
    return lax.ppermute(message, axis, pairs) if pairs else jnp.zeros_like(message)


def is_even(axis):
    return lax.rem(lax.axis_index(axis), 2) == 0


def lane_group(shape):
    return lax.broadcasted_iota(jnp.int32, shape, len(shape) - 1) // TILE


def start_kernel(sides, right_ref, labels_ref, colors_ref, table_ref, own_ref, *side_refs):
    nx, ny, nz = labels_ref.shape
    own_ref[0:3] = right_ref[...]
    own_ref[3:6] = colors_ref[...].astype(jnp.float32)

    def look_up(x, carry):
        label = labels_ref[x]
        value = jnp.zeros(label.shape, jnp.float32)
        for region in range(table_ref.shape[0]):
            value = jnp.where(label == region, table_ref[region], value)
        own_ref[6, x] = value
        return carry

    lax.fori_loop(0, nx, look_up, 0)
    even = is_even("gz")
    group = lane_group((ny, nx * TILE))
    for side in range(sides):
        tail = even if side == 0 else jnp.logical_not(even)
        edge = pl.multiple_of(jnp.where(tail, nz - LANES, 0), LANES)
        turn = jnp.where(tail, TILE, 0)

        def pack(field, carry):
            packed = jnp.zeros((ny, nx * TILE), jnp.float32)
            for x in range(nx):
                row = own_ref[field, x, :, pl.ds(edge, LANES)]
                moved = pltpu.roll(row, (x * TILE) % LANES + turn, 1)
                if nx * TILE > LANES:
                    moved = jnp.tile(moved, (1, nx * TILE // LANES))
                packed = jnp.where(group == x, moved, packed)
            side_refs[side][field] = packed
            return carry

        lax.fori_loop(0, NFIELD, pack, 0)


def second_kernel(sides, own_ref, *refs):
    side_refs, (first_ref, other_ref) = refs[:sides], refs[sides:]
    nx, ny = own_ref.shape[1:3]
    even = is_even("gy")
    for out_ref, tail in ((first_ref, even), (other_ref, jnp.logical_not(even))):
        edge = pl.multiple_of(jnp.where(tail, ny - TILE, 0), TILE)
        out_ref[:, 0:nx] = own_ref[:, :, pl.ds(edge, TILE), :]
        for side in range(sides):
            out_ref[:, nx + side] = side_refs[side][:, pl.ds(edge, TILE), :]


def third_kernel(sides, own_ref, *refs):
    side_refs, (near_ref, far_ref, first_ref, other_ref) = refs[:sides], refs[sides:]
    nx, ny = own_ref.shape[1:3]
    even_y = is_even("gy")
    below = pl.multiple_of(jnp.where(even_y, TILE + ny, 0), TILE)
    above = pl.multiple_of(jnp.where(even_y, 0, TILE + ny), TILE)
    even = is_even("gx")
    for out_ref, tail in ((first_ref, even), (other_ref, jnp.logical_not(even))):
        edge = jnp.where(tail, nx - HALO, 0)
        out_ref[:, 0:HALO, TILE : TILE + ny, :] = own_ref[:, pl.ds(edge, HALO)]
        out_ref[:, 0:HALO, pl.ds(below, TILE), :] = near_ref[:, pl.ds(edge, HALO)]
        out_ref[:, 0:HALO, pl.ds(above, TILE), :] = far_ref[:, pl.ds(edge, HALO)]
        for side in range(sides):
            out_ref[:, HALO + side, TILE : TILE + ny, :] = side_refs[side][...]
            out_ref[:, HALO + side, pl.ds(below, TILE), :] = near_ref[:, nx + side]
            out_ref[:, HALO + side, pl.ds(above, TILE), :] = far_ref[:, nx + side]


def solve_kernel(
    sides, own_hbm, near_hbm, far_hbm, left_hbm, right_hbm, mine_hbm, table_ref, out_ref,
    cells, edges, inverse, inside, residue, step_dir, solved, packed, sems,
):
    nx, ny, nz = out_ref.shape[1:]
    wide = nx + 2 * HALO
    rows, lanes = cells.shape[2:]
    even_x, even_y, even_z = (is_even(axis) for axis in ("gx", "gy", "gz"))
    below = pl.multiple_of(jnp.where(even_y, TILE + ny, 0), TILE)
    above = pl.multiple_of(jnp.where(even_y, 0, TILE + ny), TILE)
    before = jnp.where(even_x, HALO + nx, 0)
    after = jnp.where(even_x, 0, HALO + nx)
    span = pl.ds(HALO, nx)
    whole = pl.ds(0, nz)
    copies = [
        (own_hbm, cells.at[:, span, pl.ds(TILE, ny), whole]),
        (near_hbm.at[:, pl.ds(0, nx)], cells.at[:, span, pl.ds(below, TILE), whole]),
        (far_hbm.at[:, pl.ds(0, nx)], cells.at[:, span, pl.ds(above, TILE), whole]),
        (left_hbm.at[:, pl.ds(0, HALO)], cells.at[:, pl.ds(before, HALO), :, whole]),
        (right_hbm.at[:, pl.ds(0, HALO)], cells.at[:, pl.ds(after, HALO), :, whole]),
    ]
    if sides:
        side_span = pl.ds(HALO, sides)
        copies += [
            (mine_hbm.at[:, side_span], packed.at[0]),
            (left_hbm.at[:, side_span], packed.at[jnp.where(even_x, 2, 1)]),
            (right_hbm.at[:, side_span], packed.at[jnp.where(even_x, 1, 2)]),
        ]
    copies = [pltpu.make_async_copy(src, dst, sems.at[n]) for n, (src, dst) in enumerate(copies)]
    for copy in copies:
        copy.start()
    for copy in copies:
        copy.wait()

    group = lane_group((rows, LANES))
    last_group = LANES // TILE - 1

    def spread(field, carry):
        for x in range(wide):
            place, source = (1, x - HALO + nx) if x < HALO else ((0, x - HALO) if x < HALO + nx else (2, x - HALO - nx))
            tail = jnp.zeros((rows, LANES), jnp.float32)
            column, group_at = divmod(source * TILE, LANES)
            for side in range(sides):
                upper = even_z if side == 0 else jnp.logical_not(even_z)
                value = packed[place, field, side, :, column * LANES : (column + 1) * LANES]
                turn = (LANES - group_at) % LANES + jnp.where(upper, 0, LANES - TILE)
                moved = pltpu.roll(value, lax.rem(turn, LANES), 1)
                tail = jnp.where(group == jnp.where(upper, 0, last_group), moved, tail)
            cells[field, x, :, nz:lanes] = tail
        return carry

    lax.fori_loop(0, NFIELD, spread, 0)

    def up_y(v):
        return pltpu.roll(v, rows - 1, 0)

    def down_y(v):
        return pltpu.roll(v, 1, 0)

    def up_z(v):
        return pltpu.roll(v, lanes - 1, 1)

    def down_z(v):
        return pltpu.roll(v, 1, 1)

    def prepare(x, carry):
        conduct = cells[6, x]
        within = conduct > 0.0
        inv = jnp.where(within, 1.0 / (16.0 + conduct), 0.0)
        inverse[x] = inv
        inside[x] = jnp.where(within, 1.0, 0.0)
        for b in range(3):
            edges[b, x] = jnp.where(cells[3 + b, x] == 0.0, cells[b, x] * inv, 0.0)
        return carry

    lax.fori_loop(0, wide, prepare, 0)

    def curl_parts(x, ex, ey, ez):
        keep = inside[x]
        face_y = (ez - edges[2, x + 1] + up_z(ex) - ex) * keep
        face_z = (ex - up_y(ex) + edges[1, x + 1] - ey) * keep
        return keep, face_y, face_z

    for turn in range(1, HALO + 1):
        color = float(turn % NCOL)
        first, last = turn, wide - turn

        def smooth(x, carry, color=color):
            old_y, old_z = carry
            ex, ey, ez = edges[0, x], edges[1, x], edges[2, x]
            keep, face_y, face_z = curl_parts(x, ex, ey, ez)
            face_x = (ey - up_z(ey) + up_y(ez) - ez) * keep
            conduct, inv = cells[6, x], inverse[x]
            back = (
                face_z - down_y(face_z) - face_y + down_z(face_y),
                face_x - down_z(face_x) - face_z + old_z,
                face_y - old_y - face_x + down_y(face_x),
            )
            for b, own in enumerate((ex, ey, ez)):
                left = cells[b, x] - (back[b] + conduct * own)
                edges[b, x] = own + jnp.where(cells[3 + b, x] == color, left * inv, 0.0)
            return face_y, face_z

        start = first - 1
        _, face_y, face_z = curl_parts(start, edges[0, start], edges[1, start], edges[2, start])
        lax.fori_loop(first, last, smooth, (face_y, face_z))

    top = table_ref[0]
    for region in range(1, table_ref.shape[0]):
        top = jnp.maximum(top, table_ref[region])
    upper = 13.0 * jnp.full((1, lanes), top, jnp.float32)
    lower = upper / 30.0
    centre = 0.5 * (upper + lower)
    half_width = 0.5 * (upper - lower)
    ratio = centre / half_width
    damping = 1.0 / ratio
    by_centre = 1.0 / centre
    reach = NCHEB - 1

    def start_nodal(x, carry):
        keep = inside[x]
        total = None
        for c in range(3):
            own = cells[c, x]
            under = cells[0, x - 1] if c == 0 else (down_y(own) if c == 1 else down_z(own))
            gap = under - own
            total = gap if c == 0 else total + gap
            mean = 0.5 * (own + under) * keep
            residue[1 + c, x] = mean
            step_dir[1 + c, x] = mean * by_centre
            solved[1 + c, x] = mean * by_centre
        total = total * keep
        residue[0, x] = total
        step_dir[0, x] = total * by_centre
        solved[0, x] = total * by_centre
        return carry

    lax.fori_loop(HALO - reach, HALO + nx + 1 + reach, start_nodal, 0)
    for turn in range(1, NCHEB):
        damping_next = 1.0 / (2.0 * ratio - damping)
        keep_by, gain = damping_next * damping, 2.0 * damping_next / half_width
        damping = damping_next
        first, last = HALO - reach + turn, HALO + nx + 1 + reach - turn

        for field in range(4):

            def chebyshev(x, old_flux, field=field, keep_by=keep_by, gain=gain):
                value, conduct = step_dir[field, x], cells[6, x]
                flux_x = conduct * (step_dir[field, x + 1] - value)
                flux_y = conduct * (up_y(value) - value)
                flux_z = conduct * (up_z(value) - value)
                summed = (
                    (old_flux - flux_x) + (down_y(flux_y) - flux_y) + (down_z(flux_z) - flux_z)
                )
                if field:
                    summed = summed + conduct * value
                rest = residue[field, x] - summed
                residue[field, x] = rest
                moved = keep_by * value + (gain * inside[x]) * rest
                step_dir[field, x] = moved
                solved[field, x] = solved[field, x] + moved
                return flux_x

            flux = cells[6, first - 1] * (step_dir[field, first] - step_dir[field, first - 1])
            lax.fori_loop(first, last, chebyshev, flux)

    def finish(x, carry):
        at = x + HALO
        node = solved[0, at]
        for c in range(3):
            mean = solved[1 + c, at]
            if c == 0:
                node_up, mean_up = solved[0, at + 1], solved[1, at + 1]
            else:
                shift = up_y if c == 1 else up_z
                node_up, mean_up = shift(node), shift(mean)
            total = edges[c, at] + ((node_up - node) + 0.5 * (mean + mean_up))
            out_ref[c, x] = total[TILE : TILE + ny, 0:nz]
        return carry

    lax.fori_loop(0, nx, finish, 0)


def on_device(right_side, labels, colors, table):
    nx, ny, nz = labels.shape
    sides = sum(1 for pairs in swaps_of(lax.axis_size("gz")) if pairs)
    vmem, smem = pl.BlockSpec(memory_space=pltpu.VMEM), pl.BlockSpec(memory_space=pltpu.SMEM)
    anywhere = pl.BlockSpec(memory_space=pl.ANY)

    def array(*shape):
        return jax.ShapeDtypeStruct(shape, jnp.float32)

    def bind(kernel):
        return lambda *refs: kernel(sides, *refs)

    own, *packed = pl.pallas_call(
        bind(start_kernel),
        out_shape=[array(NFIELD, nx, ny, nz)] + [array(NFIELD, ny, nx * TILE)] * sides,
        in_specs=[vmem, vmem, vmem, smem],
        out_specs=[vmem] * (1 + sides),
        name="pack_third",
    )(right_side, labels, colors, table)
    packed = [
        exchange(message, "gz", pairs)
        for message, pairs in zip(packed, swaps_of(lax.axis_size("gz")))
    ]
    second = pl.pallas_call(
        bind(second_kernel),
        out_shape=[array(NFIELD, nx + sides, TILE, nz)] * 2,
        in_specs=[vmem] * (1 + sides),
        out_specs=[vmem] * 2,
        name="pack_second",
    )(own, *packed)
    near, far = (
        exchange(message, "gy", pairs)
        for message, pairs in zip(second, swaps_of(lax.axis_size("gy")))
    )
    rows = ny + 2 * TILE
    first = pl.pallas_call(
        bind(third_kernel),
        out_shape=[array(NFIELD, HALO + sides, rows, nz)] * 2,
        in_specs=[vmem] * (3 + sides),
        out_specs=[vmem] * 2,
        name="pack_first",
    )(own, *packed, near, far)
    left, right = (
        exchange(message, "gx", pairs)
        for message, pairs in zip(first, swaps_of(lax.axis_size("gx")))
    )
    wide, lanes = nx + 2 * HALO, nz + LANES
    scratch = lambda *lead: pltpu.VMEM((*lead, wide, rows, lanes), jnp.float32)
    return pl.pallas_call(
        bind(solve_kernel),
        out_shape=array(3, nx, ny, nz),
        in_specs=[anywhere] * 6 + [smem],
        out_specs=vmem,
        scratch_shapes=[
            scratch(NFIELD), scratch(3), scratch(), scratch(), scratch(4), scratch(4), scratch(4),
            pltpu.VMEM((3, NFIELD, max(sides, 1), rows, nx * TILE), jnp.float32),
            pltpu.SemaphoreType.DMA((8,)),
        ],
        name="solve",
    )(own, near, far, left, right, first[0], table)


def solution(mesh):
    in_specs = (P(None, "gx", "gy", "gz"), P("gx", "gy", "gz"), P(None, "gx", "gy", "gz"), P())
    out_specs = P(None, "gx", "gy", "gz")
    return jax.shard_map(
        on_device, mesh=mesh, in_specs=in_specs, out_specs=out_specs, check_vma=False
    )
```

```python
import jax
import jax.numpy as jnp
from jax import lax
from jax.experimental import pallas as pl
from jax.experimental.pallas import tpu as pltpu
from jax.sharding import PartitionSpec as P

NSWEEP = 2
NCOL = 4
NCHEB = 4
HALO = NSWEEP * NCOL - 1
TILE = 8
LANES = 128
NFIELD = 7


def swap_pairs(count, parity):
    pairs = []
    for low in range(parity, count - 1, 2):
        pairs += [(low, low + 1), (low + 1, low)]
    return pairs


def swaps_of(count):
    return [swap_pairs(count, parity) for parity in (0, 1)]


def exchange(message, axis, pairs):
    return lax.ppermute(message, axis, pairs) if pairs else jnp.zeros_like(message)


def is_even(axis):
    return lax.rem(lax.axis_index(axis), 2) == 0


def lane_group(shape):
    return lax.broadcasted_iota(jnp.int32, shape, len(shape) - 1) // TILE


def start_kernel(sides, right_ref, labels_ref, colors_ref, table_ref, own_ref, *side_refs):
    nx, ny, nz = labels_ref.shape
    own_ref[0:3] = right_ref[...]
    own_ref[3:6] = colors_ref[...].astype(jnp.float32)

    def look_up(x, carry):
        label = labels_ref[x]
        value = jnp.zeros(label.shape, jnp.float32)
        for region in range(table_ref.shape[0]):
            value = jnp.where(label == region, table_ref[region], value)
        own_ref[6, x] = value
        return carry

    lax.fori_loop(0, nx, look_up, 0)
    even = is_even("gz")
    group = lane_group((ny, nx * TILE))
    for side in range(sides):
        tail = even if side == 0 else jnp.logical_not(even)
        edge = pl.multiple_of(jnp.where(tail, nz - LANES, 0), LANES)
        turn = jnp.where(tail, TILE, 0)

        def pack(field, carry):
            packed = jnp.zeros((ny, nx * TILE), jnp.float32)
            for x in range(nx):
                row = own_ref[field, x, :, pl.ds(edge, LANES)]
                moved = pltpu.roll(row, (x * TILE) % LANES + turn, 1)
                if nx * TILE > LANES:
                    moved = jnp.tile(moved, (1, nx * TILE // LANES))
                packed = jnp.where(group == x, moved, packed)
            side_refs[side][field] = packed
            return carry

        lax.fori_loop(0, NFIELD, pack, 0)


def second_kernel(sides, own_ref, *refs):
    side_refs, (first_ref, other_ref) = refs[:sides], refs[sides:]
    nx, ny = own_ref.shape[1:3]
    even = is_even("gy")
    for out_ref, tail in ((first_ref, even), (other_ref, jnp.logical_not(even))):
        edge = pl.multiple_of(jnp.where(tail, ny - TILE, 0), TILE)
        out_ref[:, 0:nx] = own_ref[:, :, pl.ds(edge, TILE), :]
        for side in range(sides):
            out_ref[:, nx + side] = side_refs[side][:, pl.ds(edge, TILE), :]


def third_kernel(sides, own_ref, *refs):
    side_refs, (near_ref, far_ref, first_ref, other_ref) = refs[:sides], refs[sides:]
    nx, ny = own_ref.shape[1:3]
    even_y = is_even("gy")
    below = pl.multiple_of(jnp.where(even_y, TILE + ny, 0), TILE)
    above = pl.multiple_of(jnp.where(even_y, 0, TILE + ny), TILE)
    even = is_even("gx")
    for out_ref, tail in ((first_ref, even), (other_ref, jnp.logical_not(even))):
        edge = jnp.where(tail, nx - HALO, 0)
        out_ref[:, 0:HALO, TILE : TILE + ny, :] = own_ref[:, pl.ds(edge, HALO)]
        out_ref[:, 0:HALO, pl.ds(below, TILE), :] = near_ref[:, pl.ds(edge, HALO)]
        out_ref[:, 0:HALO, pl.ds(above, TILE), :] = far_ref[:, pl.ds(edge, HALO)]
        for side in range(sides):
            out_ref[:, HALO + side, TILE : TILE + ny, :] = side_refs[side][...]
            out_ref[:, HALO + side, pl.ds(below, TILE), :] = near_ref[:, nx + side]
            out_ref[:, HALO + side, pl.ds(above, TILE), :] = far_ref[:, nx + side]


def by_parity(even, when_even, when_odd):
    return jnp.where(even, when_even, when_odd)


def neighbour_rows(ref, index, tile, shift, rows):
    if 0 <= tile + shift and tile + shift + TILE <= rows:
        return ref[index + (pl.ds(tile + shift, TILE),)]
    return pltpu.roll(ref[index + (pl.ds(tile, TILE),)], -shift % TILE, 0)


def over(first, count, body, choices=(4, 3, 5, 2)):
    unroll = min(choices, key=lambda u: (count % u) if u <= count else count)
    trips = count // unroll

    def step(trip, carry):
        for part in range(unroll):
            body(first + trip * unroll + part)
        return carry

    if trips > 1:
        lax.fori_loop(0, trips, step, 0)
    elif trips:
        step(0, 0)
    for part in range(trips * unroll, count):
        body(first + part)


class Window:
    def __init__(self, refs, table_ref):
        (self.cells, self.edges, self.edges_up, self.faces, self.faces_down, self.inverse,
         self.inside, self.conduct_down, self.weight, self.nodes, self.nodes_up,
         self.nodes_down, self.step_dir, self.rhs) = refs
        self.columns, self.rows = self.cells.shape[2:4]
        self.tiles = tuple(range(0, self.rows, TILE))
        self.own_tiles = self.tiles[1:-1]
        self.own_columns = self.columns - 1
        self.lane = lax.broadcasted_iota(jnp.int32, (TILE, LANES), 1)
        top = table_ref[0]
        for region in range(1, table_ref.shape[0]):
            top = jnp.maximum(top, table_ref[region])
        upper = 13.0 * jnp.full((TILE, LANES), top, jnp.float32)
        lower = upper / 30.0
        centre = 0.5 * (upper + lower)
        half_width = 0.5 * (upper - lower)
        ratio = centre / half_width
        damping = 1.0 / ratio
        self.by_centre = 1.0 / centre
        self.terms = []
        for _ in range(1, NCHEB):
            damping_next = 1.0 / (2.0 * ratio - damping)
            self.terms.append((damping_next * damping, 2.0 * damping_next / half_width))
            damping = damping_next

    def up_z(self, values):
        moved = [pltpu.roll(v, LANES - 1, 1) for v in values]
        return [
            jnp.where(self.lane == LANES - 1, moved[(c + 1) % len(moved)], moved[c])
            for c in range(len(moved))
        ]

    def down_z(self, values):
        moved = [pltpu.roll(v, 1, 1) for v in values]
        return [jnp.where(self.lane == 0, moved[c - 1], moved[c]) for c in range(len(moved))]

    def spread(self, field, x, sources, group_at):
        even_z = is_even("gz")
        group = self.lane // TILE
        last_group = LANES // TILE - 1
        for tile in self.tiles:
            tail = jnp.zeros((TILE, LANES), jnp.float32)
            for side, source in enumerate(sources):
                upper = even_z if side == 0 else jnp.logical_not(even_z)
                at_lane = lax.rem(group_at * TILE, LANES)
                turn = LANES - at_lane + by_parity(upper, 0, LANES - TILE)
                moved = pltpu.roll(source(tile), lax.rem(turn, LANES), 1)
                tail = jnp.where(group == by_parity(upper, 0, last_group), moved, tail)
            self.cells[field, x, self.own_columns, pl.ds(tile, TILE)] = tail

    def prepare(self, x):
        for tile in self.tiles:
            here = pl.ds(tile, TILE)
            sigma, first = [], [[], []]
            for c in range(self.columns):
                value = self.cells[6, x, c, here]
                sigma.append(value)
                within = value > 0.0
                inv = jnp.where(within, 1.0 / (16.0 + value), 0.0)
                self.inverse[x, c, here] = inv
                self.inside[x, c, here] = jnp.where(within, 1.0, 0.0)
                for b in range(3):
                    start = jnp.where(
                        self.cells[3 + b, x, c, here] == 0.0, self.cells[b, x, c, here] * inv, 0.0
                    )
                    self.edges[0, b, x, c, here] = start
                    if b < 2:
                        first[b].append(start)
            for b in range(2):
                for c, value in enumerate(self.up_z(first[b])):
                    self.edges_up[0, b, x, c, here] = value
            for c, value in enumerate(self.down_z(sigma)):
                self.conduct_down[x, c, here] = value

    def curl(self, x, old, final):
        edges, edges_up = self.edges, self.edges_up
        for tile in self.tiles[:-1] if final else self.tiles:
            here = pl.ds(tile, TILE)
            turned = [[], []]
            for c in range(self.columns):
                keep = self.inside[x, c, here]
                ex, ey, ez = (edges[old, b, x, c, here] for b in range(3))
                ex_y = neighbour_rows(edges, (old, 0, x, c), tile, 1, self.rows)
                ez_y = neighbour_rows(edges, (old, 2, x, c), tile, 1, self.rows)
                face_x = (ey - edges_up[old, 1, x, c, here] + ez_y - ez) * keep
                face_y = (ez - edges[old, 2, x + 1, c, here] + edges_up[old, 0, x, c, here] - ex) * keep
                face_z = (ex - ex_y + edges[old, 1, x + 1, c, here] - ey) * keep
                for b, face in enumerate((face_x, face_y, face_z)):
                    self.faces[b, x, c, here] = face
                    if b < 2:
                        turned[b].append(face)
            for b in range(2):
                for c, value in enumerate(self.down_z(turned[b])):
                    self.faces_down[b, x, c, here] = value

    def update(self, x, old, color, final):
        faces, faces_down = self.faces, self.faces_down
        for tile in self.own_tiles if final else self.tiles:
            here = pl.ds(tile, TILE)
            turned = [[], []]
            for c in range(self.own_columns if final else self.columns):
                inv = self.inverse[x, c, here]
                fx, fy, fz = (faces[b, x, c, here] for b in range(3))
                fx_y = neighbour_rows(faces, (0, x, c), tile, -1, self.rows)
                fz_y = neighbour_rows(faces, (2, x, c), tile, -1, self.rows)
                back = (
                    (fz - fz_y) - (fy - faces_down[1, x, c, here]),
                    (fx - faces_down[0, x, c, here]) - (fz - faces[2, x - 1, c, here]),
                    (fy - faces[1, x - 1, c, here]) - (fx - fx_y),
                )
                for b in range(3):
                    own = self.edges[old, b, x, c, here]
                    fresh = (16.0 * own + (self.cells[b, x, c, here] - back[b])) * inv
                    fresh = jnp.where(self.cells[3 + b, x, c, here] == color, fresh, own)
                    self.edges[1 - old, b, x, c, here] = fresh
                    if b < 2:
                        turned[b].append(fresh)
            if not final:
                for b in range(2):
                    for c, value in enumerate(self.up_z(turned[b])):
                        self.edges_up[1 - old, b, x, c, here] = value

    def smooth(self, turn, first, count):
        old, color, final = (turn - 1) % 2, float(turn % NCOL), turn == HALO
        over(first - 1, count + 1, lambda x: self.curl(x, old, final))
        over(first, count, lambda x: self.update(x, old, color, final))

    def start_nodal(self, x):
        cells = self.cells
        for tile in self.tiles:
            here = pl.ds(tile, TILE)
            third_down = self.down_z([cells[2, x, c, here] for c in range(self.columns)])
            parts = [[] for _ in range(4)]
            for c in range(self.columns):
                keep = self.inside[x, c, here]
                pairs = (
                    (cells[0, x, c, here], cells[0, x - 1, c, here]),
                    (cells[1, x, c, here], neighbour_rows(cells, (1, x, c), tile, -1, self.rows)),
                    (cells[2, x, c, here], third_down[c]),
                )
                gap = (pairs[0][1] - pairs[0][0]) + (pairs[1][1] - pairs[1][0])
                gap = gap + (pairs[2][1] - pairs[2][0])
                values = [gap * keep] + [(0.5 * keep) * (a + b) for a, b in pairs]
                self.weight[x, c, here] = (
                    3.0 * cells[6, x, c, here] + cells[6, x - 1, c, here]
                    + neighbour_rows(cells, (6, x, c), tile, -1, self.rows)
                    + self.conduct_down[x, c, here]
                )
                for f, value in enumerate(values):
                    self.rhs[f, x, c, here] = value
                    value = value * self.by_centre
                    self.step_dir[f, x, c, here] = value
                    self.nodes[0, f, x, c, here] = value
                    parts[f].append(value)
            for f in range(4):
                for c, value in enumerate(self.up_z(parts[f])):
                    self.nodes_up[f, x, c, here] = value
                for c, value in enumerate(self.down_z(parts[f])):
                    self.nodes_down[f, x, c, here] = value

    def chebyshev(self, x, turn):
        old, final = (turn - 1) % 2, turn == NCHEB - 1
        keep_by, gain = self.terms[turn - 1]
        nodes, cells = self.nodes, self.cells
        for tile in self.tiles[1:] if final else self.tiles:
            here = pl.ds(tile, TILE)
            parts = [[] for _ in range(4)]
            for c in range(self.columns):
                sigma, sigma_x = cells[6, x, c, here], cells[6, x - 1, c, here]
                sigma_y = neighbour_rows(cells, (6, x, c), tile, -1, self.rows)
                sigma_z = self.conduct_down[x, c, here]
                total, gained = self.weight[x, c, here], gain * self.inside[x, c, here]
                for f in range(4):
                    value = nodes[old, f, x, c, here]
                    above = nodes[old, f, x + 1, c, here] + self.nodes_up[f, x, c, here]
                    above = above + neighbour_rows(nodes, (old, f, x, c), tile, 1, self.rows)
                    below = neighbour_rows(nodes, (old, f, x, c), tile, -1, self.rows)
                    applied = (total if f == 0 else total + sigma) * value - sigma * above
                    applied = applied - sigma_x * nodes[old, f, x - 1, c, here]
                    applied = applied - sigma_y * below
                    applied = applied - sigma_z * self.nodes_down[f, x, c, here]
                    rest = self.rhs[f, x, c, here] - applied
                    moved = keep_by * self.step_dir[f, x, c, here] + gained * rest
                    value = value + moved
                    if not final:
                        self.step_dir[f, x, c, here] = moved
                    nodes[1 - old, f, x, c, here] = value
                    parts[f].append(value)
            for f in range(4):
                if not final or f in (0, 3):
                    for c, value in enumerate(self.up_z(parts[f])):
                        self.nodes_up[f, x, c, here] = value
                if not final:
                    for c, value in enumerate(self.down_z(parts[f])):
                        self.nodes_down[f, x, c, here] = value

    def nodal(self, first, count, shrink):
        over(first(0), count, self.start_nodal, (4, 2, 3))
        for turn in range(1, NCHEB):
            over(first(turn), count - shrink * turn, lambda x: self.chebyshev(x, turn), (3, 4, 2))

    def correction(self, x, tile, c):
        done, nodes = (NCHEB - 1) % 2, self.nodes
        here = pl.ds(tile, TILE)
        node = nodes[done, 0, x, c, here]
        ups = (
            (nodes[done, 0, x + 1, c, here], nodes[done, 1, x + 1, c, here]),
            tuple(neighbour_rows(nodes, (done, f, x, c), tile, 1, self.rows) for f in (0, 2)),
            (self.nodes_up[0, x, c, here], self.nodes_up[3, x, c, here]),
        )
        return [
            (node_up - node) + 0.5 * (nodes[done, 1 + b, x, c, here] + mean_up)
            for b, (node_up, mean_up) in enumerate(ups)
        ]

    def smoothed(self, x, tile, c):
        return [self.edges[HALO % 2, b, x, c, pl.ds(tile, TILE)] for b in range(3)]


def row_at(tile, c):
    return pl.ds(tile - TILE, TILE), pl.ds(c * LANES, LANES)


def inner_kernel(
    sides, own_hbm, near_hbm, far_hbm, met_hbm, mine_hbm, table_ref,
    part_ref, edges_ref, edges_up_ref, cells_ref, terms_ref, nodes_ref, shifted_ref, *rest,
):
    *arrays, packed, sems = rest
    window = Window(arrays, table_ref)
    cells = window.cells
    nx, ny, nz = part_ref.shape[1:]
    even_x, even_y = is_even("gx"), is_even("gy")
    below = pl.multiple_of(by_parity(even_y, TILE + ny, 0), TILE)
    above = pl.multiple_of(by_parity(even_y, 0, TILE + ny), TILE)
    own_at, met_at = by_parity(even_x, 0, HALO), by_parity(even_x, nx, 0)
    span = pl.ds(own_at, nx)
    copies = []
    for c in range(window.own_columns):
        z = pl.ds(c * LANES, LANES)
        copies += [
            (own_hbm.at[:, :, :, z], cells.at[:, span, c, pl.ds(TILE, ny)]),
            (near_hbm.at[:, pl.ds(0, nx), :, z], cells.at[:, span, c, pl.ds(below, TILE)]),
            (far_hbm.at[:, pl.ds(0, nx), :, z], cells.at[:, span, c, pl.ds(above, TILE)]),
            (met_hbm.at[:, pl.ds(0, HALO), :, z], cells.at[:, pl.ds(met_at, HALO), c]),
        ]
    if sides:
        copies += [
            (mine_hbm.at[:, pl.ds(HALO, sides)], packed.at[0]),
            (met_hbm.at[:, pl.ds(HALO, sides)], packed.at[1]),
        ]
    copies = [pltpu.make_async_copy(src, dst, sems.at[n]) for n, (src, dst) in enumerate(copies)]
    for copy in copies:
        copy.start()
    for copy in copies:
        copy.wait()

    met_group = by_parity(even_x, 0, nx - HALO)

    def sources(place, field, group):
        column = group * TILE // LANES if isinstance(group, int) else 0
        return [
            lambda tile, side=side: packed[
                place, field, side, pl.ds(tile, TILE), pl.ds(column * LANES, LANES)
            ]
            for side in range(sides)
        ]

    def spread(field, carry):
        for x in range(nx):
            window.spread(field, own_at + x, sources(0, field, x), x)
        for x in range(HALO):
            window.spread(field, met_at + x, sources(1, field, met_group), met_group + x)
        return carry

    lax.fori_loop(0, NFIELD, spread, 0)
    size = nx + HALO
    over(0, size, window.prepare, (2,))
    for turn in range(1, HALO + 1):
        window.smooth(turn, turn, size - 2 * turn)
    reach = NCHEB - 1
    count = nx + reach
    nodal_at = by_parity(even_x, 1, NCHEB)
    window.nodal(lambda turn: nodal_at + turn, count, 2)

    both, both_at = nx - HALO, by_parity(even_x, HALO, 0)
    alone, alone_at = HALO - NCHEB, by_parity(even_x, NCHEB, nx - HALO)

    def result(x, smoothed):
        for tile in window.own_tiles:
            for c in range(window.own_columns):
                values = window.correction(own_at + x, tile, c)
                if smoothed:
                    values = [a + b for a, b in zip(window.smoothed(own_at + x, tile, c), values)]
                for b, value in enumerate(values):
                    part_ref[(b, x) + row_at(tile, c)] = value

    over(both_at, both, lambda x: result(x, True))
    over(alone_at, alone, lambda x: result(x, False))

    edge_at = by_parity(even_x, 0, size - HALO - 1)
    edges_ref[...] = window.edges[:, :, pl.ds(edge_at, HALO + 1)]
    edges_up_ref[...] = window.edges_up[:, :, pl.ds(edge_at, HALO + 1)]
    cells_ref[...] = cells[:, pl.ds(edge_at, HALO + 1)]
    terms_ref[0] = window.inverse[pl.ds(edge_at, HALO + 1)]
    terms_ref[1] = window.inside[pl.ds(edge_at, HALO + 1)]
    terms_ref[2] = window.conduct_down[pl.ds(edge_at, HALO + 1)]
    terms_ref[3] = window.weight[pl.ds(edge_at, HALO + 1)]
    node_at = by_parity(even_x, 1, size - NCHEB)
    nodes_ref[...] = window.nodes[:, :, pl.ds(node_at, NCHEB)]
    for n, ref in enumerate((window.nodes_up, window.nodes_down, window.step_dir, window.rhs)):
        shifted_ref[n] = ref[:, pl.ds(node_at, NCHEB)]


def outer_kernel(
    sides, met_ref, part_ref, edges_ref, edges_up_ref, cells_ref, terms_ref, nodes_ref,
    shifted_ref, table_ref, out_ref, *arrays,
):
    window = Window(arrays, table_ref)
    cells = window.cells
    nx = out_ref.shape[1]
    even_x = is_even("gx")
    size = 2 * HALO + 2
    met_at = by_parity(even_x, 0, size - HALO)
    edge_at = by_parity(even_x, HALO, 1)
    window.edges[:, :, pl.ds(edge_at, HALO + 1)] = edges_ref[...]
    window.edges_up[:, :, pl.ds(edge_at, HALO + 1)] = edges_up_ref[...]
    cells[:, pl.ds(edge_at, HALO + 1)] = cells_ref[...]
    window.inverse[pl.ds(edge_at, HALO + 1)] = terms_ref[0]
    window.inside[pl.ds(edge_at, HALO + 1)] = terms_ref[1]
    window.conduct_down[pl.ds(edge_at, HALO + 1)] = terms_ref[2]
    window.weight[pl.ds(edge_at, HALO + 1)] = terms_ref[3]
    node_at = by_parity(even_x, HALO + 1, HALO + 2 - NCHEB)
    window.nodes[:, :, pl.ds(node_at, NCHEB)] = nodes_ref[...]
    for n, ref in enumerate((window.nodes_up, window.nodes_down, window.step_dir, window.rhs)):
        ref[:, pl.ds(node_at, NCHEB)] = shifted_ref[n]
    for c in range(window.own_columns):
        cells[:, pl.ds(met_at, HALO), c] = met_ref[:, 0:HALO, :, c * LANES : (c + 1) * LANES]
    met_group = by_parity(even_x, nx - HALO, 0)

    def spread(field, carry):
        sources = [
            lambda tile, side=side: met_ref[field, HALO + side, pl.ds(tile, TILE), 0:LANES]
            for side in range(sides)
        ]
        for x in range(HALO):
            window.spread(field, met_at + x, sources, met_group + x)
        return carry

    lax.fori_loop(0, NFIELD, spread, 0)
    over(met_at, HALO, window.prepare, (HALO,))
    for turn in range(1, HALO + 1):
        window.smooth(turn, by_parity(even_x, turn, HALO + 2 - turn), HALO)
    start = by_parity(even_x, HALO + 1 - NCHEB, HALO + 2)
    window.nodal(lambda turn: by_parity(even_x, start + turn, start - turn), NCHEB, 0)

    own_at = by_parity(even_x, HALO, 2 + HALO - nx)
    both, both_at = nx - HALO, by_parity(even_x, HALO, 0)
    alone, alone_at = HALO - NCHEB, by_parity(even_x, NCHEB, nx - HALO)
    rest_at = by_parity(even_x, 0, nx - NCHEB)
    out_ref[:, pl.ds(both_at, both)] = part_ref[:, pl.ds(both_at, both)]

    def result(x, corrected):
        for tile in window.own_tiles:
            for c in range(window.own_columns):
                at = row_at(tile, c)
                if corrected:
                    values = [part_ref[(b, x) + at] for b in range(3)]
                else:
                    values = window.correction(own_at + x, tile, c)
                for b, value in enumerate(window.smoothed(own_at + x, tile, c)):
                    out_ref[(b, x) + at] = value + values[b]

    over(alone_at, alone, lambda x: result(x, True))
    over(rest_at, NCHEB, lambda x: result(x, False))


def on_device(right_side, labels, colors, table):
    nx, ny, nz = labels.shape
    sides = sum(1 for pairs in swaps_of(lax.axis_size("gz")) if pairs)
    vmem, smem = pl.BlockSpec(memory_space=pltpu.VMEM), pl.BlockSpec(memory_space=pltpu.SMEM)
    anywhere = pl.BlockSpec(memory_space=pl.ANY)

    def array(*shape):
        return jax.ShapeDtypeStruct(shape, jnp.float32)

    def call(kernel, name, outs, in_specs, scratch=(), limit=12, flops=0):
        return pl.pallas_call(
            lambda *refs: kernel(sides, *refs),
            out_shape=outs,
            in_specs=in_specs,
            out_specs=jax.tree.map(lambda _: vmem, outs),
            scratch_shapes=scratch,
            compiler_params=pltpu.CompilerParams(vmem_limit_bytes=limit << 20),
            cost_estimate=pl.CostEstimate(flops=flops, bytes_accessed=1 << 20, transcendentals=0),
            name=name,
        )

    own, *packed = call(
        start_kernel, "pack_third",
        [array(NFIELD, nx, ny, nz)] + [array(NFIELD, ny, nx * TILE)] * sides,
        [vmem, vmem, vmem, smem], limit=8,
    )(right_side, labels, colors, table)
    packed = [
        exchange(message, "gz", pairs)
        for message, pairs in zip(packed, swaps_of(lax.axis_size("gz")))
    ]
    second = call(
        second_kernel, "pack_second", [array(NFIELD, nx + sides, TILE, nz)] * 2,
        [vmem] * (1 + sides), limit=8,
    )(own, *packed)
    near, far = (
        exchange(message, "gy", pairs)
        for message, pairs in zip(second, swaps_of(lax.axis_size("gy")))
    )
    rows = ny + 2 * TILE
    first = call(
        third_kernel, "pack_first", [array(NFIELD, HALO + sides, rows, nz)] * 2,
        [vmem] * (3 + sides),
    )(own, *packed, near, far)
    met, late = (
        exchange(message, "gx", pairs)
        for message, pairs in zip(first, swaps_of(lax.axis_size("gx")))
    )
    columns = nz // LANES + 1

    def slices(*lead, depth):
        return (*lead, depth, columns, rows, LANES)

    def arrays(depth):
        leads = (
            (NFIELD,), (2, 3), (2, 2), (3,), (2,), (), (), (), (), (2, 4), (4,), (4,), (4,), (4,)
        )
        return [pltpu.VMEM(slices(*lead, depth=depth), jnp.float32) for lead in leads]

    edge, node = HALO + 1, NCHEB
    state = call(
        inner_kernel, "solve_inner",
        [
            array(3, nx, ny, nz), array(*slices(2, 3, depth=edge)),
            array(*slices(2, 2, depth=edge)), array(*slices(NFIELD, depth=edge)),
            array(*slices(4, depth=edge)), array(*slices(2, 4, depth=node)),
            array(*slices(4, 4, depth=node)),
        ],
        [anywhere] * 5 + [smem],
        arrays(nx + HALO) + [
            pltpu.VMEM((2, NFIELD, max(sides, 1), rows, nx * TILE), jnp.float32),
            pltpu.SemaphoreType.DMA((4 * (columns - 1) + 2,)),
        ],
        limit=40, flops=1 << 34,
    )(own, near, far, met, first[0], table)
    return call(
        outer_kernel, "solve_outer", array(3, nx, ny, nz), [vmem] * 8 + [smem],
        arrays(2 * HALO + 2), limit=30,
    )(late, *state, table)


def solution(mesh):
    in_specs = (P(None, "gx", "gy", "gz"), P("gx", "gy", "gz"), P(None, "gx", "gy", "gz"), P())
    out_specs = P(None, "gx", "gy", "gz")
    return jax.shard_map(
        on_device, mesh=mesh, in_specs=in_specs, out_specs=out_specs, check_vma=False
    )
```

```python
import jax
import jax.numpy as jnp
from jax import lax
from jax.experimental import pallas as pl
from jax.experimental.pallas import tpu as pltpu
from jax.sharding import PartitionSpec as P

NSWEEP = 2
NCOL = 4
NCHEB = 4
HALO = NSWEEP * NCOL - 1
TILE = 8
LANES = 128
NFIELD = 7

CURL_UNROLL, UPDATE_UNROLL = (8, 7, 6, 5), (8, 7, 6, 5)
START_UNROLL, NODAL_UNROLL, PREPARE_UNROLL = (2, 3), (3, 2), (2,)

START_LIMIT = 61


def swap_pairs(count, parity):
    pairs = []
    for low in range(parity, count - 1, 2):
        pairs += [(low, low + 1), (low + 1, low)]
    return pairs


def swaps_of(count):
    return [swap_pairs(count, parity) for parity in (0, 1)]


def joint_pairs(first, second, count):
    return [(a * count + c, b * count + d) for a, b in first for c, d in second]


def exchange(message, axis, pairs):
    return lax.ppermute(message, axis, pairs) if pairs else jnp.zeros_like(message)


def is_even(axis):
    return lax.rem(lax.axis_index(axis), 2) == 0


def lane_group(shape):
    return lax.broadcasted_iota(jnp.int32, shape, len(shape) - 1) // TILE


def start_kernel(sides, right_hbm, labels_hbm, colors_hbm, table_ref, own_ref, first_ref, other_ref, labels_ref, colors_ref, sems):
    copies = [
        pltpu.make_async_copy(labels_hbm, labels_ref, sems.at[0]),
        pltpu.make_async_copy(colors_hbm, colors_ref, sems.at[1]),
        pltpu.make_async_copy(right_hbm, own_ref.at[pl.ds(0, 3)], sems.at[2]),
    ]
    for copy in copies:
        copy.start()
    nx, ny, nz = labels_ref.shape
    copies[0].wait()

    def look_up(x, carry):
        label = labels_ref[x]
        value = jnp.zeros(label.shape, jnp.float32)
        for region in range(table_ref.shape[0]):
            value = jnp.where(label == region, table_ref[region], value)
        own_ref[6, x] = value
        return carry

    lax.fori_loop(0, nx, look_up, 0)
    copies[1].wait()
    own_ref[3:6] = colors_ref[...].astype(jnp.float32)
    copies[2].wait()
    even = is_even("gy")
    for out_ref, tail in ((first_ref, even), (other_ref, jnp.logical_not(even))):
        edge = pl.multiple_of(jnp.where(tail, ny - TILE, 0), TILE)
        out_ref[...] = own_ref[:, :, pl.ds(edge, TILE), :]


def side_kernel(sides, own_ref, *refs):
    nx, ny, nz = own_ref.shape[1:]
    even, even_y = is_even("gz"), is_even("gy")
    group = lane_group((ny, nx * TILE))
    for side in range(sides):
        packed_ref, first_ref, other_ref = refs[side::sides]
        tail = even if side == 0 else jnp.logical_not(even)
        edge = pl.multiple_of(jnp.where(tail, nz - LANES, 0), LANES)
        turn = jnp.where(tail, TILE, 0)
        for field in range(NFIELD):
            packed = jnp.zeros((ny, nx * TILE), jnp.float32)
            for x in range(nx):
                row = own_ref[field, x, :, pl.ds(edge, LANES)]
                moved = pltpu.roll(row, (x * TILE) % LANES + turn, 1)
                if nx * TILE > LANES:
                    moved = jnp.tile(moved, (1, nx * TILE // LANES))
                packed = jnp.where(group == x, moved, packed)
            packed_ref[field] = packed
        for out_ref, tail_y in ((first_ref, even_y), (other_ref, jnp.logical_not(even_y))):
            edge = pl.multiple_of(jnp.where(tail_y, ny - TILE, 0), TILE)
            out_ref[...] = packed_ref[:, pl.ds(edge, TILE), :]


def third_kernel(sides, own_ref, near_ref, far_ref, *refs):
    first_ref, other_ref = refs[3 * sides :]
    nx, ny = own_ref.shape[1:3]
    even_y = is_even("gy")
    below = pl.multiple_of(jnp.where(even_y, TILE + ny, 0), TILE)
    above = pl.multiple_of(jnp.where(even_y, 0, TILE + ny), TILE)
    even = is_even("gx")
    for out_ref, tail in ((first_ref, even), (other_ref, jnp.logical_not(even))):
        edge = jnp.where(tail, nx - HALO, 0)
        out_ref[:, 0:HALO, TILE : TILE + ny, :] = own_ref[:, pl.ds(edge, HALO)]
        out_ref[:, 0:HALO, pl.ds(below, TILE), :] = near_ref[:, pl.ds(edge, HALO)]
        out_ref[:, 0:HALO, pl.ds(above, TILE), :] = far_ref[:, pl.ds(edge, HALO)]
        for side in range(sides):
            side_ref, corner_ref, far_corner_ref = refs[side : 3 * sides : sides]
            out_ref[:, HALO + side, TILE : TILE + ny, :] = side_ref[...]
            out_ref[:, HALO + side, pl.ds(below, TILE), :] = corner_ref[...]
            out_ref[:, HALO + side, pl.ds(above, TILE), :] = far_corner_ref[...]


def by_parity(even, when_even, when_odd):
    return jnp.where(even, when_even, when_odd)


def neighbour_rows(ref, index, tile, shift, rows):
    if 0 <= tile + shift and tile + shift + TILE <= rows:
        return ref[index + (pl.ds(tile + shift, TILE),)]
    return pltpu.roll(ref[index + (pl.ds(tile, TILE),)], -shift % TILE, 0)


def over(first, count, body, choices=(4, 3, 5, 2)):
    unroll = min(choices, key=lambda u: (count % u) if u <= count else count)
    trips = count // unroll

    def step(trip, carry):
        for part in range(unroll):
            body(first + trip * unroll + part)
        return carry

    if trips > 1:
        lax.fori_loop(0, trips, step, 0)
    elif trips:
        step(0, 0)
    for part in range(trips * unroll, count):
        body(first + part)


class Window:
    def __init__(self, refs, table_ref):
        (self.cells, self.edges, self.edges_up, self.faces, self.faces_down, self.inverse,
         self.inside, self.conduct_down, self.weight, self.nodes, self.nodes_up,
         self.nodes_down, self.step_dir, self.rhs) = refs
        self.columns, self.rows = self.cells.shape[2:4]
        self.tiles = tuple(range(0, self.rows, TILE))
        self.own_tiles = self.tiles[1:-1]
        self.node_rows = self.nodes.shape[4]
        self.node_tiles = tuple(range(0, self.node_rows, TILE))
        self.own_columns = self.columns - 1
        self.lane = lax.broadcasted_iota(jnp.int32, (TILE, LANES), 1)
        top = table_ref[0]
        for region in range(1, table_ref.shape[0]):
            top = jnp.maximum(top, table_ref[region])
        upper = 13.0 * jnp.full((TILE, LANES), top, jnp.float32)
        lower = upper / 30.0
        centre = 0.5 * (upper + lower)
        half_width = 0.5 * (upper - lower)
        ratio = centre / half_width
        damping = 1.0 / ratio
        self.by_centre = 1.0 / centre
        self.terms = []
        for _ in range(1, NCHEB):
            damping_next = 1.0 / (2.0 * ratio - damping)
            self.terms.append((damping_next * damping, 2.0 * damping_next / half_width))
            damping = damping_next

    def up_z(self, values):
        moved = [pltpu.roll(v, LANES - 1, 1) for v in values]
        return [
            jnp.where(self.lane == LANES - 1, moved[(c + 1) % len(moved)], moved[c])
            for c in range(len(moved))
        ]

    def down_z(self, values):
        moved = [pltpu.roll(v, 1, 1) for v in values]
        return [jnp.where(self.lane == 0, moved[c - 1], moved[c]) for c in range(len(moved))]

    def spread(self, field, x, sources, group_at):
        even_z = is_even("gz")
        group = self.lane // TILE
        last_group = LANES // TILE - 1
        for tile in self.tiles:
            tail = jnp.zeros((TILE, LANES), jnp.float32)
            for side, source in enumerate(sources):
                upper = even_z if side == 0 else jnp.logical_not(even_z)
                at_lane = lax.rem(group_at * TILE, LANES)
                turn = LANES - at_lane + by_parity(upper, 0, LANES - TILE)
                moved = pltpu.roll(source(tile), lax.rem(turn, LANES), 1)
                tail = jnp.where(group == by_parity(upper, 0, last_group), moved, tail)
            self.cells[field, x, self.own_columns, pl.ds(tile, TILE)] = tail

    def prepare(self, x):
        for tile in self.tiles:
            here = pl.ds(tile, TILE)
            sigma, first = [], [[], []]
            for c in range(self.columns):
                value = self.cells[6, x, c, here]
                sigma.append(value)
                within = value > 0.0
                inv = jnp.where(within, 1.0 / (16.0 + value), 0.0)
                self.inverse[x, c, here] = inv
                self.inside[x, c, here] = jnp.where(within, 1.0, 0.0)
                for b in range(3):
                    start = jnp.where(
                        self.cells[3 + b, x, c, here] == 0.0, self.cells[b, x, c, here] * inv, 0.0
                    )
                    self.edges[0, b, x, c, here] = start
                    if b < 2:
                        first[b].append(start)
            for b in range(2):
                for c, value in enumerate(self.up_z(first[b])):
                    self.edges_up[0, b, x, c, here] = value
            for c, value in enumerate(self.down_z(sigma)):
                self.conduct_down[x, c, here] = value

    def curl(self, x, old, final):
        edges, edges_up = self.edges, self.edges_up
        for tile in self.tiles[:-1] if final else self.tiles:
            here = pl.ds(tile, TILE)
            turned = [[], []]
            for c in range(self.columns):
                keep = self.inside[x, c, here]
                ex, ey, ez = (edges[old, b, x, c, here] for b in range(3))
                ex_y = neighbour_rows(edges, (old, 0, x, c), tile, 1, self.rows)
                ez_y = neighbour_rows(edges, (old, 2, x, c), tile, 1, self.rows)
                face_x = (ey - edges_up[old, 1, x, c, here] + ez_y - ez) * keep
                face_y = (ez - edges[old, 2, x + 1, c, here] + edges_up[old, 0, x, c, here] - ex) * keep
                face_z = (ex - ex_y + edges[old, 1, x + 1, c, here] - ey) * keep
                for b, face in enumerate((face_x, face_y, face_z)):
                    self.faces[b, x, c, here] = face
                    if b < 2:
                        turned[b].append(face)
            for b in range(2):
                for c, value in enumerate(self.down_z(turned[b])):
                    self.faces_down[b, x, c, here] = value

    def update(self, x, old, color, final):
        faces, faces_down = self.faces, self.faces_down
        for tile in self.own_tiles if final else self.tiles:
            here = pl.ds(tile, TILE)
            turned = [[], []]
            for c in range(self.own_columns if final else self.columns):
                inv = self.inverse[x, c, here]
                fx, fy, fz = (faces[b, x, c, here] for b in range(3))
                fx_y = neighbour_rows(faces, (0, x, c), tile, -1, self.rows)
                fz_y = neighbour_rows(faces, (2, x, c), tile, -1, self.rows)
                back = (
                    (fz - fz_y) - (fy - faces_down[1, x, c, here]),
                    (fx - faces_down[0, x, c, here]) - (fz - faces[2, x - 1, c, here]),
                    (fy - faces[1, x - 1, c, here]) - (fx - fx_y),
                )
                for b in range(3):
                    own = self.edges[old, b, x, c, here]
                    fresh = (16.0 * own + (self.cells[b, x, c, here] - back[b])) * inv
                    fresh = jnp.where(self.cells[3 + b, x, c, here] == color, fresh, own)
                    self.edges[1 - old, b, x, c, here] = fresh
                    if b < 2:
                        turned[b].append(fresh)
            if not final:
                for b in range(2):
                    for c, value in enumerate(self.up_z(turned[b])):
                        self.edges_up[1 - old, b, x, c, here] = value

    def smooth(self, turn, first, count):
        old, color, final = (turn - 1) % 2, float(turn % NCOL), turn == HALO
        over(first - 1, count + 1, lambda x: self.curl(x, old, final), CURL_UNROLL)
        over(first, count, lambda x: self.update(x, old, color, final), UPDATE_UNROLL)

    def start_nodal(self, x):
        cells = self.cells
        for tile in self.node_tiles:
            here, row = pl.ds(tile, TILE), tile + TILE - NCHEB
            at, under = pl.ds(row, TILE), pl.ds(row - 1, TILE)
            third_down = self.down_z([cells[2, x, c, at] for c in range(self.columns)])
            parts = [[] for _ in range(4)]
            for c in range(self.columns):
                keep = self.inside[x, c, at]
                pairs = (
                    (cells[0, x, c, at], cells[0, x - 1, c, at]),
                    (cells[1, x, c, at], cells[1, x, c, under]),
                    (cells[2, x, c, at], third_down[c]),
                )
                gap = (pairs[0][1] - pairs[0][0]) + (pairs[1][1] - pairs[1][0])
                gap = gap + (pairs[2][1] - pairs[2][0])
                values = [gap * keep] + [(0.5 * keep) * (a + b) for a, b in pairs]
                self.weight[x, c, here] = (
                    3.0 * cells[6, x, c, at] + cells[6, x - 1, c, at]
                    + cells[6, x, c, under]
                    + self.conduct_down[x, c, at]
                )
                for f, value in enumerate(values):
                    self.rhs[f, x, c, here] = value
                    value = value * self.by_centre
                    self.step_dir[f, x, c, here] = value
                    self.nodes[0, f, x, c, here] = value
                    parts[f].append(value)
            for f in range(4):
                for c, value in enumerate(self.up_z(parts[f])):
                    self.nodes_up[f, x, c, here] = value
                for c, value in enumerate(self.down_z(parts[f])):
                    self.nodes_down[f, x, c, here] = value

    def chebyshev(self, x, turn):
        old, final = (turn - 1) % 2, turn == NCHEB - 1
        keep_by, gain = self.terms[turn - 1]
        nodes, cells = self.nodes, self.cells
        for tile in self.node_tiles:
            here, row = pl.ds(tile, TILE), tile + TILE - NCHEB
            at, under = pl.ds(row, TILE), pl.ds(row - 1, TILE)
            parts = [[] for _ in range(4)]
            for c in range(self.columns):
                sigma, sigma_x = cells[6, x, c, at], cells[6, x - 1, c, at]
                sigma_y = cells[6, x, c, under]
                sigma_z = self.conduct_down[x, c, at]
                total, gained = self.weight[x, c, here], gain * self.inside[x, c, at]
                for f in range(4):
                    value = nodes[old, f, x, c, here]
                    above = nodes[old, f, x + 1, c, here] + self.nodes_up[f, x, c, here]
                    above = above + neighbour_rows(nodes, (old, f, x, c), tile, 1, self.node_rows)
                    below = neighbour_rows(nodes, (old, f, x, c), tile, -1, self.node_rows)
                    applied = (total if f == 0 else total + sigma) * value - sigma * above
                    applied = applied - sigma_x * nodes[old, f, x - 1, c, here]
                    applied = applied - sigma_y * below
                    applied = applied - sigma_z * self.nodes_down[f, x, c, here]
                    rest = self.rhs[f, x, c, here] - applied
                    moved = keep_by * self.step_dir[f, x, c, here] + gained * rest
                    value = value + moved
                    if not final:
                        self.step_dir[f, x, c, here] = moved
                    nodes[1 - old, f, x, c, here] = value
                    parts[f].append(value)
            for f in range(4):
                if not final or f in (0, 3):
                    for c, value in enumerate(self.up_z(parts[f])):
                        self.nodes_up[f, x, c, here] = value
                if not final:
                    for c, value in enumerate(self.down_z(parts[f])):
                        self.nodes_down[f, x, c, here] = value

    def nodal(self, first, count, shrink):
        over(first(0), count, self.start_nodal, START_UNROLL)
        for turn in range(1, NCHEB):
            over(first(turn), count - shrink * turn, lambda x: self.chebyshev(x, turn), NODAL_UNROLL)

    def correction(self, x, tile, c):
        done, nodes = (NCHEB - 1) % 2, self.nodes
        row = tile - TILE + NCHEB
        here = pl.ds(row, TILE)
        node = nodes[done, 0, x, c, here]
        ups = (
            (nodes[done, 0, x + 1, c, here], nodes[done, 1, x + 1, c, here]),
            tuple(nodes[done, f, x, c, pl.ds(row + 1, TILE)] for f in (0, 2)),
            (self.nodes_up[0, x, c, here], self.nodes_up[3, x, c, here]),
        )
        return [
            (node_up - node) + 0.5 * (nodes[done, 1 + b, x, c, here] + mean_up)
            for b, (node_up, mean_up) in enumerate(ups)
        ]

    def smoothed(self, x, tile, c):
        return [self.edges[HALO % 2, b, x, c, pl.ds(tile, TILE)] for b in range(3)]


def row_at(tile, c):
    return pl.ds(tile - TILE, TILE), pl.ds(c * LANES, LANES)


def inner_kernel(
    sides, own_hbm, near_hbm, far_hbm, met_hbm, mine_hbm, table_ref,
    part_ref, edges_ref, edges_up_ref, cells_ref, terms_ref, weight_ref, nodes_ref, shifted_ref, *rest,
):
    *arrays, packed, sems = rest
    window = Window(arrays, table_ref)
    cells = window.cells
    nx, ny, nz = part_ref.shape[1:]
    even_x, even_y = is_even("gx"), is_even("gy")
    below = pl.multiple_of(by_parity(even_y, TILE + ny, 0), TILE)
    above = pl.multiple_of(by_parity(even_y, 0, TILE + ny), TILE)
    own_at, met_at = by_parity(even_x, 0, HALO), by_parity(even_x, nx, 0)
    span = pl.ds(own_at, nx)
    copies = []
    for c in range(window.own_columns):
        z = pl.ds(c * LANES, LANES)
        copies += [
            (own_hbm.at[:, :, :, z], cells.at[:, span, c, pl.ds(TILE, ny)]),
            (near_hbm.at[:, :, :, z], cells.at[:, span, c, pl.ds(below, TILE)]),
            (far_hbm.at[:, :, :, z], cells.at[:, span, c, pl.ds(above, TILE)]),
            (met_hbm.at[:, pl.ds(0, HALO), :, z], cells.at[:, pl.ds(met_at, HALO), c]),
        ]
    if sides:
        copies += [
            (mine_hbm.at[:, pl.ds(HALO, sides)], packed.at[0]),
            (met_hbm.at[:, pl.ds(HALO, sides)], packed.at[1]),
        ]
    copies = [pltpu.make_async_copy(src, dst, sems.at[n]) for n, (src, dst) in enumerate(copies)]
    for copy in copies:
        copy.start()
    for copy in copies:
        copy.wait()

    met_group = by_parity(even_x, 0, nx - HALO)

    def sources(place, field, group):
        column = group * TILE // LANES if isinstance(group, int) else 0
        return [
            lambda tile, side=side: packed[
                place, field, side, pl.ds(tile, TILE), pl.ds(column * LANES, LANES)
            ]
            for side in range(sides)
        ]

    def spread(field, carry):
        for x in range(nx):
            window.spread(field, own_at + x, sources(0, field, x), x)
        for x in range(HALO):
            window.spread(field, met_at + x, sources(1, field, met_group), met_group + x)
        return carry

    lax.fori_loop(0, NFIELD, spread, 0)
    size = nx + HALO
    over(0, size, window.prepare, PREPARE_UNROLL)
    for turn in range(1, HALO + 1):
        window.smooth(turn, turn, size - 2 * turn)
    reach = NCHEB - 1
    count = nx + reach
    nodal_at = by_parity(even_x, 1, NCHEB)
    window.nodal(lambda turn: nodal_at + turn, count, 2)

    both, both_at = nx - HALO, by_parity(even_x, HALO, 0)
    alone, alone_at = HALO - NCHEB, by_parity(even_x, NCHEB, nx - HALO)

    def result(x, smoothed):
        for tile in window.own_tiles:
            for c in range(window.own_columns):
                values = window.correction(own_at + x, tile, c)
                if smoothed:
                    values = [a + b for a, b in zip(window.smoothed(own_at + x, tile, c), values)]
                for b, value in enumerate(values):
                    part_ref[(b, x) + row_at(tile, c)] = value

    over(both_at, both, lambda x: result(x, True))
    over(alone_at, alone, lambda x: result(x, False))

    edge_at = by_parity(even_x, 0, size - HALO - 1)
    edges_ref[...] = window.edges[:, :, pl.ds(edge_at, HALO + 1)]
    edges_up_ref[...] = window.edges_up[:, :, pl.ds(edge_at, HALO + 1)]
    cells_ref[...] = cells[:, pl.ds(edge_at, HALO + 1)]
    terms_ref[0] = window.inverse[pl.ds(edge_at, HALO + 1)]
    terms_ref[1] = window.inside[pl.ds(edge_at, HALO + 1)]
    terms_ref[2] = window.conduct_down[pl.ds(edge_at, HALO + 1)]
    node_at = by_parity(even_x, 1, size - NCHEB)
    weight_ref[...] = window.weight[pl.ds(node_at, NCHEB)]
    nodes_ref[...] = window.nodes[:, :, pl.ds(node_at, NCHEB)]
    for n, ref in enumerate((window.nodes_up, window.nodes_down, window.step_dir, window.rhs)):
        shifted_ref[n] = ref[:, pl.ds(node_at, NCHEB)]


def outer_kernel(
    sides, met_ref, part_ref, edges_ref, edges_up_ref, cells_ref, terms_ref, weight_ref,
    nodes_ref, shifted_ref, table_ref, out_ref, *arrays,
):
    window = Window(arrays, table_ref)
    cells = window.cells
    nx = out_ref.shape[1]
    even_x = is_even("gx")
    size = 2 * HALO + 2
    met_at = by_parity(even_x, 0, size - HALO)
    edge_at = by_parity(even_x, HALO, 1)
    window.edges[:, :, pl.ds(edge_at, HALO + 1)] = edges_ref[...]
    window.edges_up[:, :, pl.ds(edge_at, HALO + 1)] = edges_up_ref[...]
    cells[:, pl.ds(edge_at, HALO + 1)] = cells_ref[...]
    window.inverse[pl.ds(edge_at, HALO + 1)] = terms_ref[0]
    window.inside[pl.ds(edge_at, HALO + 1)] = terms_ref[1]
    window.conduct_down[pl.ds(edge_at, HALO + 1)] = terms_ref[2]
    node_at = by_parity(even_x, HALO + 1, HALO + 2 - NCHEB)
    window.weight[pl.ds(node_at, NCHEB)] = weight_ref[...]
    window.nodes[:, :, pl.ds(node_at, NCHEB)] = nodes_ref[...]
    for n, ref in enumerate((window.nodes_up, window.nodes_down, window.step_dir, window.rhs)):
        ref[:, pl.ds(node_at, NCHEB)] = shifted_ref[n]
    for c in range(window.own_columns):
        cells[:, pl.ds(met_at, HALO), c] = met_ref[:, 0:HALO, :, c * LANES : (c + 1) * LANES]
    met_group = by_parity(even_x, nx - HALO, 0)

    def spread(field, carry):
        sources = [
            lambda tile, side=side: met_ref[field, HALO + side, pl.ds(tile, TILE), 0:LANES]
            for side in range(sides)
        ]
        for x in range(HALO):
            window.spread(field, met_at + x, sources, met_group + x)
        return carry

    lax.fori_loop(0, NFIELD, spread, 0)
    over(met_at, HALO, window.prepare, (HALO,))
    for turn in range(1, HALO + 1):
        window.smooth(turn, by_parity(even_x, turn, HALO + 2 - turn), HALO)
    start = by_parity(even_x, HALO + 1 - NCHEB, HALO + 2)
    window.nodal(lambda turn: by_parity(even_x, start + turn, start - turn), NCHEB, 0)

    own_at = by_parity(even_x, HALO, 2 + HALO - nx)
    both, both_at = nx - HALO, by_parity(even_x, HALO, 0)
    alone, alone_at = HALO - NCHEB, by_parity(even_x, NCHEB, nx - HALO)
    rest_at = by_parity(even_x, 0, nx - NCHEB)
    out_ref[:, pl.ds(both_at, both)] = part_ref[:, pl.ds(both_at, both)]

    def result(x, corrected):
        for tile in window.own_tiles:
            for c in range(window.own_columns):
                at = row_at(tile, c)
                if corrected:
                    values = [part_ref[(b, x) + at] for b in range(3)]
                else:
                    values = window.correction(own_at + x, tile, c)
                for b, value in enumerate(window.smoothed(own_at + x, tile, c)):
                    out_ref[(b, x) + at] = value + values[b]

    over(alone_at, alone, lambda x: result(x, True))
    over(rest_at, NCHEB, lambda x: result(x, False))


def on_device(right_side, labels, colors, table):
    nx, ny, nz = labels.shape
    sides = sum(1 for pairs in swaps_of(lax.axis_size("gz")) if pairs)
    vmem, smem = pl.BlockSpec(memory_space=pltpu.VMEM), pl.BlockSpec(memory_space=pltpu.SMEM)
    anywhere = pl.BlockSpec(memory_space=pl.ANY)

    def array(*shape):
        return jax.ShapeDtypeStruct(shape, jnp.float32)

    def call(kernel, name, outs, in_specs, scratch=(), limit=12, flops=0):
        return pl.pallas_call(
            lambda *refs: kernel(sides, *refs),
            out_shape=outs,
            in_specs=in_specs,
            out_specs=jax.tree.map(lambda _: vmem, outs),
            scratch_shapes=scratch,
            compiler_params=pltpu.CompilerParams(vmem_limit_bytes=limit << 20),
            cost_estimate=pl.CostEstimate(flops=flops, bytes_accessed=1 << 20, transcendentals=0),
            name=name,
        )

    hbm = pl.BlockSpec(memory_space=pltpu.HBM)
    own, *second = call(
        start_kernel, "start", [array(NFIELD, nx, ny, nz)] + [array(NFIELD, nx, TILE, nz)] * 2,
        [hbm, hbm, hbm, smem],
        [
            pltpu.VMEM((nx, ny, nz), jnp.int32), pltpu.VMEM((3, nx, ny, nz), jnp.int32),
            pltpu.SemaphoreType.DMA((3,)),
        ],
        limit=START_LIMIT,
    )(right_side, labels, colors, table)
    along_y, along_z = swaps_of(lax.axis_size("gy")), swaps_of(lax.axis_size("gz"))[:sides]
    near, far = (exchange(message, "gy", pairs) for message, pairs in zip(second, along_y))
    thirds = call(
        side_kernel, "pack_third",
        [array(NFIELD, ny, nx * TILE)] * sides + [array(NFIELD, TILE, nx * TILE)] * (2 * sides),
        [vmem],
    )(own)
    corners = [
        exchange(message, ("gy", "gz"), joint_pairs(pairs, across, lax.axis_size("gz")))
        for message, (pairs, across) in zip(
            thirds[sides:], [(pairs, across) for pairs in along_y for across in along_z]
        )
    ]
    thirds = [exchange(message, "gz", pairs) for message, pairs in zip(thirds, along_z)]
    rows = ny + 2 * TILE
    first = call(
        third_kernel, "pack_first", [array(NFIELD, HALO + sides, rows, nz)] * 2,
        [vmem] * (3 + 3 * sides), limit=14,
    )(own, near, far, *thirds, *corners)
    met, late = (
        exchange(message, "gx", pairs)
        for message, pairs in zip(first, swaps_of(lax.axis_size("gx")))
    )
    columns = nz // LANES + 1

    node_rows = ny + 2 * NCHEB

    def slices(*lead, depth, rows=rows):
        return (*lead, depth, columns, rows, LANES)

    def arrays(depth):
        shapes = [(lead, rows) for lead in ((NFIELD,), (2, 3), (2, 2), (3,), (2,), (), (), ())]
        shapes += [(lead, node_rows) for lead in ((), (2, 4), (4,), (4,), (4,), (4,))]
        return [
            pltpu.VMEM(slices(*lead, depth=depth, rows=rows), jnp.float32) for lead, rows in shapes
        ]

    edge, node = HALO + 1, NCHEB
    state = call(
        inner_kernel, "solve_inner",
        [
            array(3, nx, ny, nz), array(*slices(2, 3, depth=edge)),
            array(*slices(2, 2, depth=edge)), array(*slices(NFIELD, depth=edge)),
            array(*slices(3, depth=edge)), array(*slices(depth=node, rows=node_rows)),
            array(*slices(2, 4, depth=node, rows=node_rows)),
            array(*slices(4, 4, depth=node, rows=node_rows)),
        ],
        [anywhere] * 5 + [smem],
        arrays(nx + HALO) + [
            pltpu.VMEM((2, NFIELD, max(sides, 1), rows, nx * TILE), jnp.float32),
            pltpu.SemaphoreType.DMA((4 * (columns - 1) + 2,)),
        ],
        limit=40, flops=1 << 34,
    )(own, near, far, met, first[0], table)
    return call(
        outer_kernel, "solve_outer", array(3, nx, ny, nz), [vmem] * 9 + [smem],
        arrays(2 * HALO + 2), limit=30,
    )(late, *state, table)


def solution(mesh):
    in_specs = (P(None, "gx", "gy", "gz"), P("gx", "gy", "gz"), P(None, "gx", "gy", "gz"), P())
    out_specs = P(None, "gx", "gy", "gz")
    return jax.shard_map(
        on_device, mesh=mesh, in_specs=in_specs, out_specs=out_specs, check_vma=False
    )
```

```python
import jax
import jax.numpy as jnp
from jax import lax
from jax.experimental import pallas as pl
from jax.experimental.pallas import tpu as pltpu
from jax.sharding import PartitionSpec as P


NSWEEP = 2
NCOL = 4
NCHEB = 4
HALO = NSWEEP * NCOL - 1
TILE = 8
LANES = 128
NFIELD = 7

CURL_UNROLL, UPDATE_UNROLL = (8, 7, 6, 5), (4, 3, 5)
START_UNROLL, NODAL_UNROLL, PREPARE_UNROLL = (2, 3), (5, 4, 3), (4, 3)

START_LIMIT = 61


def swap_pairs(count, parity):
    pairs = []
    for low in range(parity, count - 1, 2):
        pairs += [(low, low + 1), (low + 1, low)]
    return pairs


def swaps_of(count):
    return [swap_pairs(count, parity) for parity in (0, 1)]


def joint_pairs(first, second, count):
    return [(a * count + c, b * count + d) for a, b in first for c, d in second]


def exchange(message, axis, pairs):
    return lax.ppermute(message, axis, pairs) if pairs else jnp.zeros_like(message)


def is_even(axis):
    return lax.rem(lax.axis_index(axis), 2) == 0


def lane_group(shape):
    return lax.broadcasted_iota(jnp.int32, shape, len(shape) - 1) // TILE


def start_kernel(sides, right_hbm, labels_hbm, colors_hbm, table_ref, own_ref, first_ref, other_ref, labels_ref, colors_ref, sems):
    copies = [
        pltpu.make_async_copy(labels_hbm, labels_ref, sems.at[0]),
        pltpu.make_async_copy(colors_hbm, colors_ref, sems.at[1]),
        pltpu.make_async_copy(right_hbm, own_ref.at[pl.ds(0, 3)], sems.at[2]),
    ]
    for copy in copies:
        copy.start()
    nx, ny, _ = labels_ref.shape
    copies[0].wait()

    def look_up(x, carry):
        label = labels_ref[x]
        value = jnp.zeros(label.shape, jnp.float32)
        for region in range(table_ref.shape[0]):
            value = jnp.where(label == region, table_ref[region], value)
        own_ref[6, x] = value
        return carry

    lax.fori_loop(0, nx, look_up, 0)
    copies[1].wait()
    own_ref[3:6] = colors_ref[...].astype(jnp.float32)
    copies[2].wait()
    even = is_even("gy")
    for out_ref, tail in ((first_ref, even), (other_ref, jnp.logical_not(even))):
        edge = pl.multiple_of(jnp.where(tail, ny - TILE, 0), TILE)
        out_ref[...] = own_ref[:, :, pl.ds(edge, TILE), :]


def side_kernel(sides, own_ref, *refs):
    nx, ny, nz = own_ref.shape[1:]
    *refs, low_ref, high_ref = refs
    low_ref[...] = own_ref[:, 0:HALO]
    high_ref[...] = own_ref[:, nx - HALO : nx]
    even, even_y = is_even("gz"), is_even("gy")
    group = lane_group((ny, nx * TILE))
    for side in range(sides):
        packed_ref, first_ref, other_ref = refs[side::sides]
        tail = even if side == 0 else jnp.logical_not(even)
        edge = pl.multiple_of(jnp.where(tail, nz - LANES, 0), LANES)
        turn = jnp.where(tail, TILE, 0)
        for field in range(NFIELD):
            packed = jnp.zeros((ny, nx * TILE), jnp.float32)
            for x in range(nx):
                row = own_ref[field, x, :, pl.ds(edge, LANES)]
                moved = pltpu.roll(row, (x * TILE) % LANES + turn, 1)
                if nx * TILE > LANES:
                    moved = jnp.tile(moved, (1, nx * TILE // LANES))
                packed = jnp.where(group == x, moved, packed)
            packed_ref[field] = packed
        for out_ref, tail_y in ((first_ref, even_y), (other_ref, jnp.logical_not(even_y))):
            edge = pl.multiple_of(jnp.where(tail_y, ny - TILE, 0), TILE)
            out_ref[...] = packed_ref[:, pl.ds(edge, TILE), :]


def third_kernel(sides, low_ref, high_ref, near_ref, far_ref, *refs):
    first_ref, other_ref = refs[3 * sides :]
    nx, ny = near_ref.shape[1], low_ref.shape[2]
    even_y = is_even("gy")
    below = pl.multiple_of(jnp.where(even_y, TILE + ny, 0), TILE)
    above = pl.multiple_of(jnp.where(even_y, 0, TILE + ny), TILE)
    even = is_even("gx")
    for out_ref, tail in ((first_ref, even), (other_ref, jnp.logical_not(even))):
        edge = jnp.where(tail, nx - HALO, 0)
        for end_ref, chosen in ((high_ref, tail), (low_ref, jnp.logical_not(tail))):

            @pl.when(chosen)
            def _(end_ref=end_ref, out_ref=out_ref):
                out_ref[:, 0:HALO, TILE : TILE + ny, :] = end_ref[...]

        out_ref[:, 0:HALO, pl.ds(below, TILE), :] = near_ref[:, pl.ds(edge, HALO)]
        out_ref[:, 0:HALO, pl.ds(above, TILE), :] = far_ref[:, pl.ds(edge, HALO)]
        for side in range(sides):
            side_ref, corner_ref, far_corner_ref = refs[side : 3 * sides : sides]
            out_ref[:, HALO + side, TILE : TILE + ny, :] = side_ref[...]
            out_ref[:, HALO + side, pl.ds(below, TILE), :] = corner_ref[...]
            out_ref[:, HALO + side, pl.ds(above, TILE), :] = far_corner_ref[...]


def by_parity(even, when_even, when_odd):
    return jnp.where(even, when_even, when_odd)


def neighbour_rows(ref, index, tile, shift, rows):
    if 0 <= tile + shift and tile + shift + TILE <= rows:
        return ref[index + (pl.ds(tile + shift, TILE),)]
    return pltpu.roll(ref[index + (pl.ds(tile, TILE),)], -shift % TILE, 0)


def over(first, count, body, choices=(4, 3, 5, 2)):
    unroll = min(choices, key=lambda u: (count % u) if u <= count else count)
    trips = count // unroll

    def step(trip, carry):
        for part in range(unroll):
            body(first + trip * unroll + part)
        return carry

    if trips > 1:
        lax.fori_loop(0, trips, step, 0)
    elif trips:
        step(0, 0)
    for part in range(trips * unroll, count):
        body(first + part)


class Window:
    def __init__(self, refs, table_ref):
        (self.cells, self.edges, self.edges_up, self.faces, self.faces_down, self.inverse,
         self.inside, self.conduct_down, self.weight, self.nodes, self.nodes_up,
         self.nodes_down, self.step_dir, self.rhs) = refs
        self.columns, self.rows = self.cells.shape[2:4]
        self.tiles = tuple(range(0, self.rows, TILE))
        self.own_tiles = self.tiles[1:-1]
        self.node_rows = self.nodes.shape[4]
        self.node_tiles = tuple(range(0, self.node_rows, TILE))
        self.own_columns = self.columns - 1
        self.lane = lax.broadcasted_iota(jnp.int32, (TILE, LANES), 1)
        top = table_ref[0]
        for region in range(1, table_ref.shape[0]):
            top = jnp.maximum(top, table_ref[region])
        upper = 13.0 * jnp.full((TILE, LANES), top, jnp.float32)
        lower = upper / 30.0
        centre = 0.5 * (upper + lower)
        half_width = 0.5 * (upper - lower)
        ratio = centre / half_width
        damping = 1.0 / ratio
        self.by_centre = 1.0 / centre
        self.terms = []
        for _ in range(1, NCHEB):
            damping_next = 1.0 / (2.0 * ratio - damping)
            self.terms.append((damping_next * damping, 2.0 * damping_next / half_width))
            damping = damping_next

    def up_z(self, values):
        moved = [pltpu.roll(v, LANES - 1, 1) for v in values]
        return [
            jnp.where(self.lane == LANES - 1, moved[(c + 1) % len(moved)], moved[c])
            for c in range(len(moved))
        ]

    def down_z(self, values):
        moved = [pltpu.roll(v, 1, 1) for v in values]
        return [jnp.where(self.lane == 0, moved[c - 1], moved[c]) for c in range(len(moved))]

    def spread(self, field, x, sources, group_at):
        even_z = is_even("gz")
        group = self.lane // TILE
        last_group = LANES // TILE - 1
        for tile in self.tiles:
            tail = jnp.zeros((TILE, LANES), jnp.float32)
            for side, source in enumerate(sources):
                upper = even_z if side == 0 else jnp.logical_not(even_z)
                at_lane = lax.rem(group_at * TILE, LANES)
                turn = LANES - at_lane + by_parity(upper, 0, LANES - TILE)
                moved = pltpu.roll(source(tile), lax.rem(turn, LANES), 1)
                tail = jnp.where(group == by_parity(upper, 0, last_group), moved, tail)
            self.cells[field, x, self.own_columns, pl.ds(tile, TILE)] = tail

    def prepare(self, x):
        for tile in self.tiles:
            here = pl.ds(tile, TILE)
            sigma, first = [], [[], []]
            for c in range(self.columns):
                value = self.cells[6, x, c, here]
                sigma.append(value)
                within = value > 0.0
                inv = jnp.where(within, 1.0 / (16.0 + value), 0.0)
                self.inverse[x, c, here] = inv
                self.inside[x, c, here] = jnp.where(within, 1.0, 0.0)
                for b in range(3):
                    start = jnp.where(
                        self.cells[3 + b, x, c, here] == 0.0, self.cells[b, x, c, here] * inv, 0.0
                    )
                    self.edges[0, b, x, c, here] = start
                    if b < 2:
                        first[b].append(start)
            for b in range(2):
                for c, value in enumerate(self.up_z(first[b])):
                    self.edges_up[0, b, x, c, here] = value
            for c, value in enumerate(self.down_z(sigma)):
                self.conduct_down[x, c, here] = value

    def curl(self, x, old, final):
        edges, edges_up = self.edges, self.edges_up
        for tile in self.tiles[:-1] if final else self.tiles:
            here = pl.ds(tile, TILE)
            turned = [[], []]
            for c in range(self.columns):
                keep = self.inside[x, c, here]
                ex, ey, ez = (edges[old, b, x, c, here] for b in range(3))
                ex_y = neighbour_rows(edges, (old, 0, x, c), tile, 1, self.rows)
                ez_y = neighbour_rows(edges, (old, 2, x, c), tile, 1, self.rows)
                face_x = (ey - edges_up[old, 1, x, c, here] + ez_y - ez) * keep
                face_y = (ez - edges[old, 2, x + 1, c, here] + edges_up[old, 0, x, c, here] - ex) * keep
                face_z = (ex - ex_y + edges[old, 1, x + 1, c, here] - ey) * keep
                for b, face in enumerate((face_x, face_y, face_z)):
                    self.faces[b, x, c, here] = face
                    if b < 2:
                        turned[b].append(face)
            for b in range(2):
                for c, value in enumerate(self.down_z(turned[b])):
                    self.faces_down[b, x, c, here] = value

    def update(self, x, old, color, final):
        faces, faces_down = self.faces, self.faces_down
        for tile in self.own_tiles if final else self.tiles:
            here = pl.ds(tile, TILE)
            turned = [[], []]
            for c in range(self.own_columns if final else self.columns):
                inv = self.inverse[x, c, here]
                fx, fy, fz = (faces[b, x, c, here] for b in range(3))
                fx_y = neighbour_rows(faces, (0, x, c), tile, -1, self.rows)
                fz_y = neighbour_rows(faces, (2, x, c), tile, -1, self.rows)
                back = (
                    (fz - fz_y) - (fy - faces_down[1, x, c, here]),
                    (fx - faces_down[0, x, c, here]) - (fz - faces[2, x - 1, c, here]),
                    (fy - faces[1, x - 1, c, here]) - (fx - fx_y),
                )
                for b in range(3):
                    own = self.edges[old, b, x, c, here]
                    fresh = (16.0 * own + (self.cells[b, x, c, here] - back[b])) * inv
                    fresh = jnp.where(self.cells[3 + b, x, c, here] == color, fresh, own)
                    self.edges[1 - old, b, x, c, here] = fresh
                    if b < 2:
                        turned[b].append(fresh)
            if not final:
                for b in range(2):
                    for c, value in enumerate(self.up_z(turned[b])):
                        self.edges_up[1 - old, b, x, c, here] = value

    def smooth(self, turn, first, count):
        old, color, final = (turn - 1) % 2, float(turn % NCOL), turn == HALO
        over(first - 1, count + 1, lambda x: self.curl(x, old, final), CURL_UNROLL)
        over(first, count, lambda x: self.update(x, old, color, final), UPDATE_UNROLL)

    def start_nodal(self, x):
        cells = self.cells
        for tile in self.node_tiles:
            here, row = pl.ds(tile, TILE), tile + TILE - NCHEB
            at, under = pl.ds(row, TILE), pl.ds(row - 1, TILE)
            third_down = self.down_z([cells[2, x, c, at] for c in range(self.columns)])
            parts = [[] for _ in range(4)]
            for c in range(self.columns):
                keep = self.inside[x, c, at]
                pairs = (
                    (cells[0, x, c, at], cells[0, x - 1, c, at]),
                    (cells[1, x, c, at], cells[1, x, c, under]),
                    (cells[2, x, c, at], third_down[c]),
                )
                gap = (pairs[0][1] - pairs[0][0]) + (pairs[1][1] - pairs[1][0])
                gap = gap + (pairs[2][1] - pairs[2][0])
                values = [gap * keep] + [(0.5 * keep) * (a + b) for a, b in pairs]
                self.weight[x, c, here] = (
                    3.0 * cells[6, x, c, at] + cells[6, x - 1, c, at]
                    + cells[6, x, c, under]
                    + self.conduct_down[x, c, at]
                )
                for f, value in enumerate(values):
                    self.rhs[f, x, c, here] = value
                    value = value * self.by_centre
                    self.step_dir[f, x, c, here] = value
                    self.nodes[0, f, x, c, here] = value
                    parts[f].append(value)
            for f in range(4):
                for c, value in enumerate(self.up_z(parts[f])):
                    self.nodes_up[f, x, c, here] = value
                for c, value in enumerate(self.down_z(parts[f])):
                    self.nodes_down[f, x, c, here] = value

    def chebyshev(self, x, turn):
        old, final = (turn - 1) % 2, turn == NCHEB - 1
        keep_by, gain = self.terms[turn - 1]
        nodes, cells = self.nodes, self.cells
        for tile in self.node_tiles:
            here, row = pl.ds(tile, TILE), tile + TILE - NCHEB
            at, under = pl.ds(row, TILE), pl.ds(row - 1, TILE)
            parts = [[] for _ in range(4)]
            for c in range(self.columns):
                sigma, sigma_x = cells[6, x, c, at], cells[6, x - 1, c, at]
                sigma_y = cells[6, x, c, under]
                sigma_z = self.conduct_down[x, c, at]
                total, gained = self.weight[x, c, here], gain * self.inside[x, c, at]
                for f in range(4):
                    value = nodes[old, f, x, c, here]
                    above = nodes[old, f, x + 1, c, here] + self.nodes_up[f, x, c, here]
                    above = above + neighbour_rows(nodes, (old, f, x, c), tile, 1, self.node_rows)
                    below = neighbour_rows(nodes, (old, f, x, c), tile, -1, self.node_rows)
                    applied = (total if f == 0 else total + sigma) * value - sigma * above
                    applied = applied - sigma_x * nodes[old, f, x - 1, c, here]
                    applied = applied - sigma_y * below
                    applied = applied - sigma_z * self.nodes_down[f, x, c, here]
                    rest = self.rhs[f, x, c, here] - applied
                    moved = keep_by * self.step_dir[f, x, c, here] + gained * rest
                    value = value + moved
                    if not final:
                        self.step_dir[f, x, c, here] = moved
                    nodes[1 - old, f, x, c, here] = value
                    parts[f].append(value)
            for f in range(4):
                if not final or f in (0, 3):
                    for c, value in enumerate(self.up_z(parts[f])):
                        self.nodes_up[f, x, c, here] = value
                if not final:
                    for c, value in enumerate(self.down_z(parts[f])):
                        self.nodes_down[f, x, c, here] = value

    def nodal(self, first, count, shrink):
        over(first(0), count, self.start_nodal, START_UNROLL)
        for turn in range(1, NCHEB):
            over(first(turn), count - shrink * turn, lambda x: self.chebyshev(x, turn), NODAL_UNROLL)

    def correction(self, x, tile, c):
        done, nodes = (NCHEB - 1) % 2, self.nodes
        row = tile - TILE + NCHEB
        here = pl.ds(row, TILE)
        node = nodes[done, 0, x, c, here]
        ups = (
            (nodes[done, 0, x + 1, c, here], nodes[done, 1, x + 1, c, here]),
            tuple(nodes[done, f, x, c, pl.ds(row + 1, TILE)] for f in (0, 2)),
            (self.nodes_up[0, x, c, here], self.nodes_up[3, x, c, here]),
        )
        return [
            (node_up - node) + 0.5 * (nodes[done, 1 + b, x, c, here] + mean_up)
            for b, (node_up, mean_up) in enumerate(ups)
        ]

    def smoothed(self, x, tile, c):
        return [self.edges[HALO % 2, b, x, c, pl.ds(tile, TILE)] for b in range(3)]


def row_at(tile, c):
    return pl.ds(tile - TILE, TILE), pl.ds(c * LANES, LANES)


def inner_kernel(
    sides, own_hbm, near_hbm, far_hbm, met_hbm, mine_hbm, table_ref,
    part_ref, edges_ref, edges_up_ref, cells_ref, terms_ref, weight_ref, nodes_ref, shifted_ref, *rest,
):
    *arrays, packed, sems = rest
    window = Window(arrays, table_ref)
    cells = window.cells
    nx, ny, _ = part_ref.shape[1:]
    even_x, even_y = is_even("gx"), is_even("gy")
    below = pl.multiple_of(by_parity(even_y, TILE + ny, 0), TILE)
    above = pl.multiple_of(by_parity(even_y, 0, TILE + ny), TILE)
    own_at, met_at = by_parity(even_x, 0, HALO), by_parity(even_x, nx, 0)
    span = pl.ds(own_at, nx)
    copies = []
    for c in range(window.own_columns):
        z = pl.ds(c * LANES, LANES)
        copies += [
            (own_hbm.at[:, :, :, z], cells.at[:, span, c, pl.ds(TILE, ny)]),
            (near_hbm.at[:, :, :, z], cells.at[:, span, c, pl.ds(below, TILE)]),
            (far_hbm.at[:, :, :, z], cells.at[:, span, c, pl.ds(above, TILE)]),
            (met_hbm.at[:, pl.ds(0, HALO), :, z], cells.at[:, pl.ds(met_at, HALO), c]),
        ]
    if sides:
        copies += [
            (mine_hbm.at[:, pl.ds(HALO, sides)], packed.at[0]),
            (met_hbm.at[:, pl.ds(HALO, sides)], packed.at[1]),
        ]
    copies = [pltpu.make_async_copy(src, dst, sems.at[n]) for n, (src, dst) in enumerate(copies)]
    for copy in copies:
        copy.start()
    for copy in copies:
        copy.wait()

    met_group = by_parity(even_x, 0, nx - HALO)

    def sources(place, field, group):
        column = group * TILE // LANES if isinstance(group, int) else 0
        return [
            lambda tile, side=side: packed[
                place, field, side, pl.ds(tile, TILE), pl.ds(column * LANES, LANES)
            ]
            for side in range(sides)
        ]

    def spread(field, carry):
        for x in range(nx):
            window.spread(field, own_at + x, sources(0, field, x), x)
        for x in range(HALO):
            window.spread(field, met_at + x, sources(1, field, met_group), met_group + x)
        return carry

    lax.fori_loop(0, NFIELD, spread, 0)
    size = nx + HALO
    over(0, size, window.prepare, PREPARE_UNROLL)
    for turn in range(1, HALO + 1):
        window.smooth(turn, turn, size - 2 * turn)
    reach = NCHEB - 1
    count = nx + reach
    nodal_at = by_parity(even_x, 1, NCHEB)
    window.nodal(lambda turn: nodal_at + turn, count, 2)

    both, both_at = nx - HALO, by_parity(even_x, HALO, 0)
    alone, alone_at = HALO - NCHEB, by_parity(even_x, NCHEB, nx - HALO)

    def result(x, smoothed):
        for tile in window.own_tiles:
            for c in range(window.own_columns):
                values = window.correction(own_at + x, tile, c)
                if smoothed:
                    values = [a + b for a, b in zip(window.smoothed(own_at + x, tile, c), values)]
                for b, value in enumerate(values):
                    part_ref[(b, x) + row_at(tile, c)] = value

    over(both_at, both, lambda x: result(x, True))
    over(alone_at, alone, lambda x: result(x, False))

    edge_at = by_parity(even_x, 0, size - HALO - 1)
    edges_ref[...] = window.edges[:, :, pl.ds(edge_at, HALO + 1)]
    edges_up_ref[...] = window.edges_up[:, :, pl.ds(edge_at, HALO + 1)]
    cells_ref[...] = cells[:, pl.ds(edge_at, HALO + 1)]
    terms_ref[0] = window.inverse[pl.ds(edge_at, HALO + 1)]
    terms_ref[1] = window.inside[pl.ds(edge_at, HALO + 1)]
    terms_ref[2] = window.conduct_down[pl.ds(edge_at, HALO + 1)]
    node_at = by_parity(even_x, 1, size - NCHEB)
    weight_ref[...] = window.weight[pl.ds(node_at, NCHEB)]
    nodes_ref[...] = window.nodes[:, :, pl.ds(node_at, NCHEB)]
    for n, ref in enumerate((window.nodes_up, window.nodes_down, window.step_dir, window.rhs)):
        shifted_ref[n] = ref[:, pl.ds(node_at, NCHEB)]


def outer_kernel(
    sides, met_ref, part_ref, edges_ref, edges_up_ref, cells_ref, terms_ref, weight_ref,
    nodes_ref, shifted_ref, table_ref, out_ref, *arrays,
):
    window = Window(arrays, table_ref)
    cells = window.cells
    nx = out_ref.shape[1]
    even_x = is_even("gx")
    size = 2 * HALO + 2
    met_at = by_parity(even_x, 0, size - HALO)
    edge_at = by_parity(even_x, HALO, 1)
    window.edges[:, :, pl.ds(edge_at, HALO + 1)] = edges_ref[...]
    window.edges_up[:, :, pl.ds(edge_at, HALO + 1)] = edges_up_ref[...]
    cells[:, pl.ds(edge_at, HALO + 1)] = cells_ref[...]
    window.inverse[pl.ds(edge_at, HALO + 1)] = terms_ref[0]
    window.inside[pl.ds(edge_at, HALO + 1)] = terms_ref[1]
    window.conduct_down[pl.ds(edge_at, HALO + 1)] = terms_ref[2]
    node_at = by_parity(even_x, HALO + 1, HALO + 2 - NCHEB)
    window.weight[pl.ds(node_at, NCHEB)] = weight_ref[...]
    window.nodes[:, :, pl.ds(node_at, NCHEB)] = nodes_ref[...]
    for n, ref in enumerate((window.nodes_up, window.nodes_down, window.step_dir, window.rhs)):
        ref[:, pl.ds(node_at, NCHEB)] = shifted_ref[n]
    for c in range(window.own_columns):
        cells[:, pl.ds(met_at, HALO), c] = met_ref[:, 0:HALO, :, c * LANES : (c + 1) * LANES]
    met_group = by_parity(even_x, nx - HALO, 0)

    def spread(field, carry):
        sources = [
            lambda tile, side=side: met_ref[field, HALO + side, pl.ds(tile, TILE), 0:LANES]
            for side in range(sides)
        ]
        for x in range(HALO):
            window.spread(field, met_at + x, sources, met_group + x)
        return carry

    lax.fori_loop(0, NFIELD, spread, 0)
    over(met_at, HALO, window.prepare, (HALO,))
    for turn in range(1, HALO + 1):
        window.smooth(turn, by_parity(even_x, turn, HALO + 2 - turn), HALO)
    start = by_parity(even_x, HALO + 1 - NCHEB, HALO + 2)
    window.nodal(lambda turn: by_parity(even_x, start + turn, start - turn), NCHEB, 0)

    own_at = by_parity(even_x, HALO, 2 + HALO - nx)
    both, both_at = nx - HALO, by_parity(even_x, HALO, 0)
    alone, alone_at = HALO - NCHEB, by_parity(even_x, NCHEB, nx - HALO)
    rest_at = by_parity(even_x, 0, nx - NCHEB)
    out_ref[:, pl.ds(both_at, both)] = part_ref[:, pl.ds(both_at, both)]

    def result(x, corrected):
        for tile in window.own_tiles:
            for c in range(window.own_columns):
                at = row_at(tile, c)
                if corrected:
                    values = [part_ref[(b, x) + at] for b in range(3)]
                else:
                    values = window.correction(own_at + x, tile, c)
                for b, value in enumerate(window.smoothed(own_at + x, tile, c)):
                    out_ref[(b, x) + at] = value + values[b]

    over(alone_at, alone, lambda x: result(x, True))
    over(rest_at, NCHEB, lambda x: result(x, False))


def on_device(right_side, labels, colors, table):
    nx, ny, nz = labels.shape
    sides = sum(1 for pairs in swaps_of(lax.axis_size("gz")) if pairs)
    vmem, smem = pl.BlockSpec(memory_space=pltpu.VMEM), pl.BlockSpec(memory_space=pltpu.SMEM)
    anywhere = pl.BlockSpec(memory_space=pl.ANY)

    def array(*shape):
        return jax.ShapeDtypeStruct(shape, jnp.float32)

    def call(kernel, outs, in_specs, scratch=(), limit=12, flops=0):
        return pl.pallas_call(
            lambda *refs: kernel(sides, *refs),
            out_shape=outs,
            in_specs=in_specs,
            out_specs=jax.tree.map(lambda _: vmem, outs),
            scratch_shapes=scratch,
            compiler_params=pltpu.CompilerParams(vmem_limit_bytes=limit << 20),
            cost_estimate=pl.CostEstimate(flops=flops, bytes_accessed=1 << 20, transcendentals=0),
        )

    hbm = pl.BlockSpec(memory_space=pltpu.HBM)
    own, *second = call(
        start_kernel, [array(NFIELD, nx, ny, nz)] + [array(NFIELD, nx, TILE, nz)] * 2,
        [hbm, hbm, hbm, smem],
        [
            pltpu.VMEM((nx, ny, nz), jnp.int32), pltpu.VMEM((3, nx, ny, nz), jnp.int32),
            pltpu.SemaphoreType.DMA((3,)),
        ],
        limit=START_LIMIT,
    )(right_side, labels, colors, table)
    along_y, along_z = swaps_of(lax.axis_size("gy")), swaps_of(lax.axis_size("gz"))[:sides]
    far = exchange(second[1], "gy", along_y[1])
    near = exchange(second[0], "gy", along_y[0])
    *thirds, low, high = call(
        side_kernel,
        [array(NFIELD, ny, nx * TILE)] * sides + [array(NFIELD, TILE, nx * TILE)] * (2 * sides)
        + [array(NFIELD, HALO, ny, nz)] * 2,
        [vmem],
    )(own)
    corners = [
        exchange(message, ("gy", "gz"), joint_pairs(pairs, across, lax.axis_size("gz")))
        for message, (pairs, across) in zip(
            thirds[sides:], [(pairs, across) for pairs in along_y for across in along_z]
        )
    ]
    thirds = [exchange(message, "gz", pairs) for message, pairs in zip(thirds, along_z)]
    rows = ny + 2 * TILE
    first = call(
        third_kernel, [array(NFIELD, HALO + sides, rows, nz)] * 2,
        [vmem] * (4 + 3 * sides), limit=14,
    )(low, high, near, far, *thirds, *corners)
    along_x = swaps_of(lax.axis_size("gx"))
    late = exchange(first[1], "gx", along_x[1])
    met = exchange(first[0], "gx", along_x[0])
    columns = nz // LANES + 1

    node_rows = ny + 2 * NCHEB

    def slices(*lead, depth, rows=rows):
        return (*lead, depth, columns, rows, LANES)

    def arrays(depth):
        shapes = [(lead, rows) for lead in ((NFIELD,), (2, 3), (2, 2), (3,), (2,), (), (), ())]
        shapes += [(lead, node_rows) for lead in ((), (2, 4), (4,), (4,), (4,), (4,))]
        return [
            pltpu.VMEM(slices(*lead, depth=depth, rows=rows), jnp.float32) for lead, rows in shapes
        ]

    edge, node = HALO + 1, NCHEB
    state = call(
        inner_kernel,
        [
            array(3, nx, ny, nz), array(*slices(2, 3, depth=edge)),
            array(*slices(2, 2, depth=edge)), array(*slices(NFIELD, depth=edge)),
            array(*slices(3, depth=edge)), array(*slices(depth=node, rows=node_rows)),
            array(*slices(2, 4, depth=node, rows=node_rows)),
            array(*slices(4, 4, depth=node, rows=node_rows)),
        ],
        [anywhere] * 5 + [smem],
        arrays(nx + HALO) + [
            pltpu.VMEM((2, NFIELD, max(sides, 1), rows, nx * TILE), jnp.float32),
            pltpu.SemaphoreType.DMA((4 * (columns - 1) + 2,)),
        ],
        limit=40, flops=1 << 34,
    )(own, near, far, met, first[0], table)
    return call(
        outer_kernel, array(3, nx, ny, nz), [vmem] * 9 + [smem],
        arrays(2 * HALO + 2), limit=30,
    )(late, *state, table)


def solution(mesh):
    in_specs = (P(None, "gx", "gy", "gz"), P("gx", "gy", "gz"), P(None, "gx", "gy", "gz"), P())
    out_specs = P(None, "gx", "gy", "gz")

    return jax.shard_map(
        on_device, mesh=mesh, in_specs=in_specs, out_specs=out_specs, check_vma=False
    )
```

```python
import jax
import jax.numpy as jnp
from jax import lax
from jax.experimental import pallas as pl
from jax.experimental.pallas import tpu as pltpu
from jax.sharding import PartitionSpec as P

NSWEEP = 2
NCOL = 4
NCHEB = 4
HALO = NSWEEP * NCOL - 1
TILE = 8
LANES = 128
NFIELD = 7

CURL_UNROLL, UPDATE_UNROLL = (8, 7, 6, 5), (4, 3, 5)
START_UNROLL, NODAL_UNROLL, PREPARE_UNROLL = (2, 3), (5, 4, 3), (4, 3)

START_LIMIT = 61


def swap_pairs(count, parity):
    pairs = []
    for low in range(parity, count - 1, 2):
        pairs += [(low, low + 1), (low + 1, low)]
    return pairs


def swaps_of(count):
    return [swap_pairs(count, parity) for parity in (0, 1)]


def joint_pairs(first, second, count):
    return [(a * count + c, b * count + d) for a, b in first for c, d in second]


def exchange(message, axis, pairs):
    return lax.ppermute(message, axis, pairs) if pairs else jnp.zeros_like(message)


def is_even(axis):
    return lax.rem(lax.axis_index(axis), 2) == 0


def lane_group(shape):
    return lax.broadcasted_iota(jnp.int32, shape, len(shape) - 1) // TILE


def start_kernel(
    sides, right_hbm, labels_hbm, colors_hbm, table_ref, own_hbm, first_hbm, other_hbm,
    labels_ref, colors_ref, own_ref, sems, out_sems,
):
    nx, ny, nz = labels_ref.shape
    copies = [
        pltpu.make_async_copy(labels_hbm, labels_ref, sems.at[0]),
        pltpu.make_async_copy(right_hbm, own_ref.at[pl.ds(0, 3)], sems.at[1]),
        pltpu.make_async_copy(colors_hbm, colors_ref, sems.at[2]),
    ]
    for copy in copies:
        copy.start()
    even = is_even("gy")
    high, low = pl.multiple_of(by_parity(even, ny - TILE, 0), TILE), pl.multiple_of(by_parity(even, 0, ny - TILE), TILE)
    sent = []

    def send(begin, count):
        fields = pl.ds(begin, count)
        for target, source in (
            (first_hbm, own_ref.at[fields, :, pl.ds(high, TILE)]),
            (other_hbm, own_ref.at[fields, :, pl.ds(low, TILE)]),
            (own_hbm, own_ref.at[fields]),
        ):
            copy = pltpu.make_async_copy(source, target.at[fields], out_sems.at[len(sent)])
            copy.start()
            sent.append(copy)

    copies[1].wait()
    send(0, 3)
    copies[2].wait()
    own_ref[3:6] = colors_ref[...].astype(jnp.float32)
    copies[0].wait()

    def look_up(x, carry):
        label = labels_ref[x]
        value = jnp.zeros(label.shape, jnp.float32)
        for region in range(table_ref.shape[0]):
            value = jnp.where(label == region, table_ref[region], value)
        own_ref[6, x] = value
        return carry

    lax.fori_loop(0, nx, look_up, 0)
    send(3, 3)
    for copy in sent[:3]:
        copy.wait()
    send(6, 1)
    for copy in sent[3:]:
        copy.wait()


def side_kernel(sides, own_ref, *refs):
    nx, ny, nz = own_ref.shape[1:]
    *refs, low_ref, high_ref = refs
    low_ref[...] = own_ref[:, 0:HALO]
    high_ref[...] = own_ref[:, nx - HALO : nx]
    even, even_y = is_even("gz"), is_even("gy")
    group = lane_group((ny, nx * TILE))
    for side in range(sides):
        packed_ref, first_ref, other_ref = refs[side::sides]
        tail = even if side == 0 else jnp.logical_not(even)
        edge = pl.multiple_of(jnp.where(tail, nz - LANES, 0), LANES)
        turn = jnp.where(tail, TILE, 0)
        for field in range(NFIELD):
            packed = jnp.zeros((ny, nx * TILE), jnp.float32)
            for x in range(nx):
                row = own_ref[field, x, :, pl.ds(edge, LANES)]
                moved = pltpu.roll(row, (x * TILE) % LANES + turn, 1)
                if nx * TILE > LANES:
                    moved = jnp.tile(moved, (1, nx * TILE // LANES))
                packed = jnp.where(group == x, moved, packed)
            packed_ref[field] = packed
        for out_ref, tail_y in ((first_ref, even_y), (other_ref, jnp.logical_not(even_y))):
            edge = pl.multiple_of(jnp.where(tail_y, ny - TILE, 0), TILE)
            out_ref[...] = packed_ref[:, pl.ds(edge, TILE), :]


def third_kernel(sides, low_ref, high_ref, near_ref, far_ref, *refs):
    first_ref, other_ref = refs[3 * sides :]
    nx, ny = near_ref.shape[1], low_ref.shape[2]
    even_y = is_even("gy")
    below = pl.multiple_of(jnp.where(even_y, TILE + ny, 0), TILE)
    above = pl.multiple_of(jnp.where(even_y, 0, TILE + ny), TILE)
    even = is_even("gx")
    for out_ref, tail in ((first_ref, even), (other_ref, jnp.logical_not(even))):
        edge = jnp.where(tail, nx - HALO, 0)
        for end_ref, chosen in ((high_ref, tail), (low_ref, jnp.logical_not(tail))):

            @pl.when(chosen)
            def _(end_ref=end_ref, out_ref=out_ref):
                out_ref[:, 0:HALO, TILE : TILE + ny, :] = end_ref[...]

        out_ref[:, 0:HALO, pl.ds(below, TILE), :] = near_ref[:, pl.ds(edge, HALO)]
        out_ref[:, 0:HALO, pl.ds(above, TILE), :] = far_ref[:, pl.ds(edge, HALO)]
        for side in range(sides):
            side_ref, corner_ref, far_corner_ref = refs[side : 3 * sides : sides]
            out_ref[:, HALO + side, TILE : TILE + ny, :] = side_ref[...]
            out_ref[:, HALO + side, pl.ds(below, TILE), :] = corner_ref[...]
            out_ref[:, HALO + side, pl.ds(above, TILE), :] = far_corner_ref[...]


def by_parity(even, when_even, when_odd):
    return jnp.where(even, when_even, when_odd)


def neighbour_rows(ref, index, tile, shift, rows):
    if 0 <= tile + shift and tile + shift + TILE <= rows:
        return ref[index + (pl.ds(tile + shift, TILE),)]
    return pltpu.roll(ref[index + (pl.ds(tile, TILE),)], -shift % TILE, 0)


def over(first, count, body, choices=(4, 3, 5, 2)):
    unroll = min(choices, key=lambda u: (count % u) if u <= count else count)
    trips = count // unroll

    def step(trip, carry):
        for part in range(unroll):
            body(first + trip * unroll + part)
        return carry

    if trips > 1:
        lax.fori_loop(0, trips, step, 0)
    elif trips:
        step(0, 0)
    for part in range(trips * unroll, count):
        body(first + part)


class Window:
    def __init__(self, refs, table_ref):
        (self.cells, self.edges, self.edges_up, self.faces, self.faces_down, self.inverse,
         self.inside, self.conduct_down, self.weight, self.nodes, self.nodes_up,
         self.nodes_down, self.step_dir, self.rhs) = refs
        self.columns, self.rows = self.cells.shape[2:4]
        self.tiles = tuple(range(0, self.rows, TILE))
        self.own_tiles = self.tiles[1:-1]
        self.node_rows = self.nodes.shape[4]
        self.node_tiles = tuple(range(0, self.node_rows, TILE))
        self.own_columns = self.columns - 1
        self.lane = lax.broadcasted_iota(jnp.int32, (TILE, LANES), 1)
        top = table_ref[0]
        for region in range(1, table_ref.shape[0]):
            top = jnp.maximum(top, table_ref[region])
        upper = 13.0 * jnp.full((TILE, LANES), top, jnp.float32)
        lower = upper / 30.0
        centre = 0.5 * (upper + lower)
        half_width = 0.5 * (upper - lower)
        ratio = centre / half_width
        damping = 1.0 / ratio
        self.by_centre = 1.0 / centre
        self.terms = []
        for _ in range(1, NCHEB):
            damping_next = 1.0 / (2.0 * ratio - damping)
            self.terms.append((damping_next * damping, 2.0 * damping_next / half_width))
            damping = damping_next

    def up_z(self, values):
        moved = [pltpu.roll(v, LANES - 1, 1) for v in values]
        return [
            jnp.where(self.lane == LANES - 1, moved[(c + 1) % len(moved)], moved[c])
            for c in range(len(moved))
        ]

    def down_z(self, values):
        moved = [pltpu.roll(v, 1, 1) for v in values]
        return [jnp.where(self.lane == 0, moved[c - 1], moved[c]) for c in range(len(moved))]

    def spread(self, field, x, sources, group_at):
        even_z = is_even("gz")
        group = self.lane // TILE
        last_group = LANES // TILE - 1
        for tile in self.tiles:
            tail = jnp.zeros((TILE, LANES), jnp.float32)
            for side, source in enumerate(sources):
                upper = even_z if side == 0 else jnp.logical_not(even_z)
                at_lane = lax.rem(group_at * TILE, LANES)
                turn = LANES - at_lane + by_parity(upper, 0, LANES - TILE)
                moved = pltpu.roll(source(tile), lax.rem(turn, LANES), 1)
                tail = jnp.where(group == by_parity(upper, 0, last_group), moved, tail)
            self.cells[field, x, self.own_columns, pl.ds(tile, TILE)] = tail

    def prepare(self, x):
        for tile in self.tiles:
            here = pl.ds(tile, TILE)
            sigma, first = [], [[], []]
            for c in range(self.columns):
                value = self.cells[6, x, c, here]
                sigma.append(value)
                within = value > 0.0
                inv = jnp.where(within, 1.0 / (16.0 + value), 0.0)
                self.inverse[x, c, here] = inv
                self.inside[x, c, here] = jnp.where(within, 1.0, 0.0)
                for b in range(3):
                    start = jnp.where(
                        self.cells[3 + b, x, c, here] == 0.0, self.cells[b, x, c, here] * inv, 0.0
                    )
                    self.edges[0, b, x, c, here] = start
                    if b < 2:
                        first[b].append(start)
            for b in range(2):
                for c, value in enumerate(self.up_z(first[b])):
                    self.edges_up[0, b, x, c, here] = value
            for c, value in enumerate(self.down_z(sigma)):
                self.conduct_down[x, c, here] = value

    def curl(self, x, old, final):
        edges, edges_up = self.edges, self.edges_up
        for tile in self.tiles[:-1] if final else self.tiles:
            here = pl.ds(tile, TILE)
            turned = [[], []]
            for c in range(self.columns):
                keep = self.inside[x, c, here]
                ex, ey, ez = (edges[old, b, x, c, here] for b in range(3))
                ex_y = neighbour_rows(edges, (old, 0, x, c), tile, 1, self.rows)
                ez_y = neighbour_rows(edges, (old, 2, x, c), tile, 1, self.rows)
                face_x = (ey - edges_up[old, 1, x, c, here] + ez_y - ez) * keep
                face_y = (ez - edges[old, 2, x + 1, c, here] + edges_up[old, 0, x, c, here] - ex) * keep
                face_z = (ex - ex_y + edges[old, 1, x + 1, c, here] - ey) * keep
                for b, face in enumerate((face_x, face_y, face_z)):
                    self.faces[b, x, c, here] = face
                    if b < 2:
                        turned[b].append(face)
            for b in range(2):
                for c, value in enumerate(self.down_z(turned[b])):
                    self.faces_down[b, x, c, here] = value

    def update(self, x, old, color, final):
        faces, faces_down = self.faces, self.faces_down
        for tile in self.own_tiles if final else self.tiles:
            here = pl.ds(tile, TILE)
            turned = [[], []]
            for c in range(self.own_columns if final else self.columns):
                inv = self.inverse[x, c, here]
                fx, fy, fz = (faces[b, x, c, here] for b in range(3))
                fx_y = neighbour_rows(faces, (0, x, c), tile, -1, self.rows)
                fz_y = neighbour_rows(faces, (2, x, c), tile, -1, self.rows)
                back = (
                    (fz - fz_y) - (fy - faces_down[1, x, c, here]),
                    (fx - faces_down[0, x, c, here]) - (fz - faces[2, x - 1, c, here]),
                    (fy - faces[1, x - 1, c, here]) - (fx - fx_y),
                )
                for b in range(3):
                    own = self.edges[old, b, x, c, here]
                    fresh = (16.0 * own + (self.cells[b, x, c, here] - back[b])) * inv
                    fresh = jnp.where(self.cells[3 + b, x, c, here] == color, fresh, own)
                    self.edges[1 - old, b, x, c, here] = fresh
                    if b < 2:
                        turned[b].append(fresh)
            if not final:
                for b in range(2):
                    for c, value in enumerate(self.up_z(turned[b])):
                        self.edges_up[1 - old, b, x, c, here] = value

    def smooth(self, turn, first, count):
        old, color, final = (turn - 1) % 2, float(turn % NCOL), turn == HALO
        over(first - 1, count + 1, lambda x: self.curl(x, old, final), CURL_UNROLL)
        over(first, count, lambda x: self.update(x, old, color, final), (HALO,) if count == HALO else UPDATE_UNROLL)

    def start_nodal(self, x):
        cells = self.cells
        for tile in self.node_tiles:
            here, row = pl.ds(tile, TILE), tile + TILE - NCHEB
            at, under = pl.ds(row, TILE), pl.ds(row - 1, TILE)
            third_down = self.down_z([cells[2, x, c, at] for c in range(self.columns)])
            parts = [[] for _ in range(4)]
            for c in range(self.columns):
                keep = self.inside[x, c, at]
                pairs = (
                    (cells[0, x, c, at], cells[0, x - 1, c, at]),
                    (cells[1, x, c, at], cells[1, x, c, under]),
                    (cells[2, x, c, at], third_down[c]),
                )
                gap = (pairs[0][1] - pairs[0][0]) + (pairs[1][1] - pairs[1][0])
                gap = gap + (pairs[2][1] - pairs[2][0])
                values = [gap * keep] + [(0.5 * keep) * (a + b) for a, b in pairs]
                self.weight[x, c, here] = (
                    3.0 * cells[6, x, c, at] + cells[6, x - 1, c, at]
                    + cells[6, x, c, under]
                    + self.conduct_down[x, c, at]
                )
                for f, value in enumerate(values):
                    self.rhs[f, x, c, here] = value
                    value = value * self.by_centre
                    self.step_dir[f, x, c, here] = value
                    self.nodes[0, f, x, c, here] = value
                    parts[f].append(value)
            for f in range(4):
                for c, value in enumerate(self.up_z(parts[f])):
                    self.nodes_up[f, x, c, here] = value
                for c, value in enumerate(self.down_z(parts[f])):
                    self.nodes_down[f, x, c, here] = value

    def chebyshev(self, x, turn):
        old, final = (turn - 1) % 2, turn == NCHEB - 1
        keep_by, gain = self.terms[turn - 1]
        nodes, cells = self.nodes, self.cells
        for tile in self.node_tiles:
            here, row = pl.ds(tile, TILE), tile + TILE - NCHEB
            at, under = pl.ds(row, TILE), pl.ds(row - 1, TILE)
            parts = [[] for _ in range(4)]
            for c in range(self.columns):
                sigma, sigma_x = cells[6, x, c, at], cells[6, x - 1, c, at]
                sigma_y = cells[6, x, c, under]
                sigma_z = self.conduct_down[x, c, at]
                total, gained = self.weight[x, c, here], gain * self.inside[x, c, at]
                for f in range(4):
                    value = nodes[old, f, x, c, here]
                    above = nodes[old, f, x + 1, c, here] + self.nodes_up[f, x, c, here]
                    above = above + neighbour_rows(nodes, (old, f, x, c), tile, 1, self.node_rows)
                    below = neighbour_rows(nodes, (old, f, x, c), tile, -1, self.node_rows)
                    applied = (total if f == 0 else total + sigma) * value - sigma * above
                    applied = applied - sigma_x * nodes[old, f, x - 1, c, here]
                    applied = applied - sigma_y * below
                    applied = applied - sigma_z * self.nodes_down[f, x, c, here]
                    rest = self.rhs[f, x, c, here] - applied
                    moved = keep_by * self.step_dir[f, x, c, here] + gained * rest
                    value = value + moved
                    if not final:
                        self.step_dir[f, x, c, here] = moved
                    nodes[1 - old, f, x, c, here] = value
                    parts[f].append(value)
            for f in range(4):
                if not final or f in (0, 3):
                    for c, value in enumerate(self.up_z(parts[f])):
                        self.nodes_up[f, x, c, here] = value
                if not final:
                    for c, value in enumerate(self.down_z(parts[f])):
                        self.nodes_down[f, x, c, here] = value

    def nodal(self, first, count, shrink):
        over(first(0), count, self.start_nodal, START_UNROLL)
        for turn in range(1, NCHEB):
            over(first(turn), count - shrink * turn, lambda x: self.chebyshev(x, turn), NODAL_UNROLL)

    def correction(self, x, tile, c):
        done, nodes = (NCHEB - 1) % 2, self.nodes
        row = tile - TILE + NCHEB
        here = pl.ds(row, TILE)
        node = nodes[done, 0, x, c, here]
        ups = (
            (nodes[done, 0, x + 1, c, here], nodes[done, 1, x + 1, c, here]),
            tuple(nodes[done, f, x, c, pl.ds(row + 1, TILE)] for f in (0, 2)),
            (self.nodes_up[0, x, c, here], self.nodes_up[3, x, c, here]),
        )
        return [
            (node_up - node) + 0.5 * (nodes[done, 1 + b, x, c, here] + mean_up)
            for b, (node_up, mean_up) in enumerate(ups)
        ]

    def smoothed(self, x, tile, c):
        return [self.edges[HALO % 2, b, x, c, pl.ds(tile, TILE)] for b in range(3)]


def row_at(tile, c):
    return pl.ds(tile - TILE, TILE), pl.ds(c * LANES, LANES)


def inner_kernel(
    sides, own_hbm, near_hbm, far_hbm, met_hbm, mine_hbm, table_ref,
    part_ref, edges_ref, edges_up_ref, cells_ref, terms_ref, weight_ref, nodes_ref, shifted_ref, *rest,
):
    *arrays, packed, sems = rest
    window = Window(arrays, table_ref)
    cells = window.cells
    nx, ny, nz = part_ref.shape[1:]
    even_x, even_y = is_even("gx"), is_even("gy")
    below = pl.multiple_of(by_parity(even_y, TILE + ny, 0), TILE)
    above = pl.multiple_of(by_parity(even_y, 0, TILE + ny), TILE)
    own_at, met_at = by_parity(even_x, 0, HALO), by_parity(even_x, nx, 0)
    span = pl.ds(own_at, nx)
    copies = []
    if sides:
        copies += [
            (mine_hbm.at[:, pl.ds(HALO, sides)], packed.at[0]),
            (met_hbm.at[:, pl.ds(HALO, sides)], packed.at[1]),
        ]
    early = len(copies)
    for c in range(window.own_columns):
        z = pl.ds(c * LANES, LANES)
        copies += [
            (own_hbm.at[:, :, :, z], cells.at[:, span, c, pl.ds(TILE, ny)]),
            (near_hbm.at[:, :, :, z], cells.at[:, span, c, pl.ds(below, TILE)]),
            (far_hbm.at[:, :, :, z], cells.at[:, span, c, pl.ds(above, TILE)]),
            (met_hbm.at[:, pl.ds(0, HALO), :, z], cells.at[:, pl.ds(met_at, HALO), c]),
        ]
    copies = [pltpu.make_async_copy(src, dst, sems.at[n]) for n, (src, dst) in enumerate(copies)]
    for copy in copies:
        copy.start()
    for copy in copies[:early]:
        copy.wait()

    met_group = by_parity(even_x, 0, nx - HALO)

    def sources(place, field, group):
        column = group * TILE // LANES if isinstance(group, int) else 0
        return [
            lambda tile, side=side: packed[
                place, field, side, pl.ds(tile, TILE), pl.ds(column * LANES, LANES)
            ]
            for side in range(sides)
        ]

    def spread(field, carry):
        for x in range(nx):
            window.spread(field, own_at + x, sources(0, field, x), x)
        for x in range(HALO):
            window.spread(field, met_at + x, sources(1, field, met_group), met_group + x)
        return carry

    lax.fori_loop(0, NFIELD, spread, 0)
    for copy in copies[early:]:
        copy.wait()
    size = nx + HALO
    over(0, size, window.prepare, PREPARE_UNROLL)
    for turn in range(1, HALO + 1):
        window.smooth(turn, turn, size - 2 * turn)
    reach = NCHEB - 1
    count = nx + reach
    nodal_at = by_parity(even_x, 1, NCHEB)
    window.nodal(lambda turn: nodal_at + turn, count, 2)

    both, both_at = nx - HALO, by_parity(even_x, HALO, 0)
    alone, alone_at = HALO - NCHEB, by_parity(even_x, NCHEB, nx - HALO)

    def result(x, smoothed):
        for tile in window.own_tiles:
            for c in range(window.own_columns):
                values = window.correction(own_at + x, tile, c)
                if smoothed:
                    values = [a + b for a, b in zip(window.smoothed(own_at + x, tile, c), values)]
                for b, value in enumerate(values):
                    part_ref[(b, x) + row_at(tile, c)] = value

    over(both_at, both, lambda x: result(x, True))
    over(alone_at, alone, lambda x: result(x, False))

    edge_at = by_parity(even_x, 0, size - HALO - 1)
    edges_ref[...] = window.edges[:, :, pl.ds(edge_at, HALO + 1)]
    edges_up_ref[...] = window.edges_up[:, :, pl.ds(edge_at, HALO + 1)]
    cells_ref[...] = cells[:, pl.ds(edge_at, HALO + 1)]
    terms_ref[0] = window.inverse[pl.ds(edge_at, HALO + 1)]
    terms_ref[1] = window.inside[pl.ds(edge_at, HALO + 1)]
    terms_ref[2] = window.conduct_down[pl.ds(edge_at, HALO + 1)]
    node_at = by_parity(even_x, 1, size - NCHEB)
    weight_ref[...] = window.weight[pl.ds(node_at, NCHEB)]
    nodes_ref[...] = window.nodes[:, :, pl.ds(node_at, NCHEB)]
    for n, ref in enumerate((window.nodes_up, window.nodes_down, window.step_dir, window.rhs)):
        shifted_ref[n] = ref[:, pl.ds(node_at, NCHEB)]


def outer_kernel(
    sides, met_ref, part_ref, edges_ref, edges_up_ref, cells_ref, terms_ref, weight_ref,
    nodes_ref, shifted_ref, table_ref, out_ref, *arrays,
):
    window = Window(arrays, table_ref)
    cells = window.cells
    nx = out_ref.shape[1]
    even_x = is_even("gx")
    size = 2 * HALO + 2
    met_at = by_parity(even_x, 0, size - HALO)
    edge_at = by_parity(even_x, HALO, 1)
    window.edges[:, :, pl.ds(edge_at, HALO + 1)] = edges_ref[...]
    window.edges_up[:, :, pl.ds(edge_at, HALO + 1)] = edges_up_ref[...]
    cells[:, pl.ds(edge_at, HALO + 1)] = cells_ref[...]
    window.inverse[pl.ds(edge_at, HALO + 1)] = terms_ref[0]
    window.inside[pl.ds(edge_at, HALO + 1)] = terms_ref[1]
    window.conduct_down[pl.ds(edge_at, HALO + 1)] = terms_ref[2]
    node_at = by_parity(even_x, HALO + 1, HALO + 2 - NCHEB)
    window.weight[pl.ds(node_at, NCHEB)] = weight_ref[...]
    window.nodes[:, :, pl.ds(node_at, NCHEB)] = nodes_ref[...]
    for n, ref in enumerate((window.nodes_up, window.nodes_down, window.step_dir, window.rhs)):
        ref[:, pl.ds(node_at, NCHEB)] = shifted_ref[n]
    for c in range(window.own_columns):
        cells[:, pl.ds(met_at, HALO), c] = met_ref[:, 0:HALO, :, c * LANES : (c + 1) * LANES]
    met_group = by_parity(even_x, nx - HALO, 0)

    def spread(field, carry):
        sources = [
            lambda tile, side=side: met_ref[field, HALO + side, pl.ds(tile, TILE), 0:LANES]
            for side in range(sides)
        ]
        for x in range(HALO):
            window.spread(field, met_at + x, sources, met_group + x)
        return carry

    lax.fori_loop(0, NFIELD, spread, 0)
    over(met_at, HALO, window.prepare, (HALO,))
    for turn in range(1, HALO + 1):
        window.smooth(turn, by_parity(even_x, turn, HALO + 2 - turn), HALO)
    start = by_parity(even_x, HALO + 1 - NCHEB, HALO + 2)
    window.nodal(lambda turn: by_parity(even_x, start + turn, start - turn), NCHEB, 0)

    own_at = by_parity(even_x, HALO, 2 + HALO - nx)
    both, both_at = nx - HALO, by_parity(even_x, HALO, 0)
    alone, alone_at = HALO - NCHEB, by_parity(even_x, NCHEB, nx - HALO)
    rest_at = by_parity(even_x, 0, nx - NCHEB)
    out_ref[:, pl.ds(both_at, both)] = part_ref[:, pl.ds(both_at, both)]

    def result(x, corrected):
        for tile in window.own_tiles:
            for c in range(window.own_columns):
                at = row_at(tile, c)
                if corrected:
                    values = [part_ref[(b, x) + at] for b in range(3)]
                else:
                    values = window.correction(own_at + x, tile, c)
                for b, value in enumerate(window.smoothed(own_at + x, tile, c)):
                    out_ref[(b, x) + at] = value + values[b]

    over(alone_at, alone, lambda x: result(x, True))
    over(rest_at, NCHEB, lambda x: result(x, False))


def on_device(right_side, labels, colors, table):
    nx, ny, nz = labels.shape
    sides = sum(1 for pairs in swaps_of(lax.axis_size("gz")) if pairs)
    vmem, smem = pl.BlockSpec(memory_space=pltpu.VMEM), pl.BlockSpec(memory_space=pltpu.SMEM)
    anywhere = pl.BlockSpec(memory_space=pl.ANY)

    def array(*shape):
        return jax.ShapeDtypeStruct(shape, jnp.float32)

    def call(kernel, name, outs, in_specs, scratch=(), limit=12, flops=0, out=vmem):
        return pl.pallas_call(
            lambda *refs: kernel(sides, *refs),
            out_shape=outs,
            in_specs=in_specs,
            out_specs=jax.tree.map(lambda _: out, outs),
            scratch_shapes=scratch,
            compiler_params=pltpu.CompilerParams(vmem_limit_bytes=limit << 20),
            cost_estimate=pl.CostEstimate(flops=flops, bytes_accessed=1 << 20, transcendentals=0),
            name=name,
        )

    hbm = pl.BlockSpec(memory_space=pltpu.HBM)
    own, *second = call(
        start_kernel, "start", [array(NFIELD, nx, ny, nz)] + [array(NFIELD, nx, TILE, nz)] * 2,
        [hbm, hbm, hbm, smem],
        [
            pltpu.VMEM((nx, ny, nz), jnp.int32), pltpu.VMEM((3, nx, ny, nz), jnp.int32),
            pltpu.VMEM((NFIELD, nx, ny, nz), jnp.float32),
            pltpu.SemaphoreType.DMA((3,)), pltpu.SemaphoreType.DMA((9,)),
        ],
        limit=START_LIMIT, out=hbm,
    )(right_side, labels, colors, table)
    along_y, along_z = swaps_of(lax.axis_size("gy")), swaps_of(lax.axis_size("gz"))[:sides]
    near = exchange(second[0], "gy", along_y[0])
    far = exchange(second[1], "gy", along_y[1])
    *thirds, low, high = call(
        side_kernel, "pack_third",
        [array(NFIELD, ny, nx * TILE)] * sides + [array(NFIELD, TILE, nx * TILE)] * (2 * sides)
        + [array(NFIELD, HALO, ny, nz)] * 2,
        [vmem],
    )(own)
    corners = [
        exchange(message, ("gy", "gz"), joint_pairs(pairs, across, lax.axis_size("gz")))
        for message, (pairs, across) in zip(
            thirds[sides:], [(pairs, across) for pairs in along_y for across in along_z]
        )
    ]
    thirds = [exchange(message, "gz", pairs) for message, pairs in zip(thirds, along_z)]
    rows = ny + 2 * TILE
    first = call(
        third_kernel, "pack_first", [array(NFIELD, HALO + sides, rows, nz)] * 2,
        [vmem] * (4 + 3 * sides), limit=14,
    )(low, high, near, far, *thirds, *corners)
    along_x = swaps_of(lax.axis_size("gx"))
    met = exchange(first[0], "gx", along_x[0])
    late = exchange(first[1], "gx", along_x[1])
    columns = nz // LANES + 1

    node_rows = ny + 2 * NCHEB

    def slices(*lead, depth, rows=rows):
        return (*lead, depth, columns, rows, LANES)

    def arrays(depth):
        shapes = [(lead, rows) for lead in ((NFIELD,), (2, 3), (2, 2), (3,), (2,), (), (), ())]
        shapes += [(lead, node_rows) for lead in ((), (2, 4), (4,), (4,), (4,), (4,))]
        return [
            pltpu.VMEM(slices(*lead, depth=depth, rows=rows), jnp.float32) for lead, rows in shapes
        ]

    edge, node = HALO + 1, NCHEB
    state = call(
        inner_kernel, "solve_inner",
        [
            array(3, nx, ny, nz), array(*slices(2, 3, depth=edge)),
            array(*slices(2, 2, depth=edge)), array(*slices(NFIELD, depth=edge)),
            array(*slices(3, depth=edge)), array(*slices(depth=node, rows=node_rows)),
            array(*slices(2, 4, depth=node, rows=node_rows)),
            array(*slices(4, 4, depth=node, rows=node_rows)),
        ],
        [anywhere] * 5 + [smem],
        arrays(nx + HALO) + [
            pltpu.VMEM((2, NFIELD, max(sides, 1), rows, nx * TILE), jnp.float32),
            pltpu.SemaphoreType.DMA((4 * (columns - 1) + 2,)),
        ],
        limit=40, flops=1 << 34,
    )(own, near, far, met, first[0], table)
    return call(
        outer_kernel, "solve_outer", array(3, nx, ny, nz), [vmem] * 9 + [smem],
        arrays(2 * HALO + 2), limit=30,
    )(late, *state, table)


def solution(mesh):
    in_specs = (P(None, "gx", "gy", "gz"), P("gx", "gy", "gz"), P(None, "gx", "gy", "gz"), P())
    out_specs = P(None, "gx", "gy", "gz")
    return jax.shard_map(
        on_device, mesh=mesh, in_specs=in_specs, out_specs=out_specs, check_vma=False
    )
```

```python
import jax
import jax.numpy as jnp
from jax import lax
from jax.experimental import pallas as pl
from jax.experimental.pallas import tpu as pltpu
from jax.sharding import PartitionSpec as P

NSWEEP = 2
NCOL = 4
NCHEB = 4
HALO = NSWEEP * NCOL - 1
TILE = 8
LANES = 128
NFIELD = 7

CURL_UNROLL, UPDATE_UNROLL = (11, 10, 9, 8, 7, 12, 6), (4,)
START_UNROLL, NODAL_UNROLL, PREPARE_UNROLL = (2, 3), (5,), (4, 3)

START_LIMIT = 61


def swap_pairs(count, parity):
    pairs = []
    for low in range(parity, count - 1, 2):
        pairs += [(low, low + 1), (low + 1, low)]
    return pairs


def swaps_of(count):
    return [swap_pairs(count, parity) for parity in (0, 1)]


def joint_pairs(first, second, count):
    return [(a * count + c, b * count + d) for a, b in first for c, d in second]


def exchange(message, axis, pairs):
    return lax.ppermute(message, axis, pairs) if pairs else jnp.zeros_like(message)


def is_even(axis):
    return lax.rem(lax.axis_index(axis), 2) == 0


def lane_group(shape):
    return lax.broadcasted_iota(jnp.int32, shape, len(shape) - 1) // TILE


def start_kernel(
    sides, right_hbm, labels_hbm, colors_hbm, table_ref, own_hbm, first_hbm, other_hbm,
    labels_ref, colors_ref, own_ref, sems, out_sems,
):
    nx, ny, nz = labels_ref.shape
    copies = [
        pltpu.make_async_copy(labels_hbm, labels_ref, sems.at[0]),
        pltpu.make_async_copy(right_hbm, own_ref.at[pl.ds(0, 3)], sems.at[1]),
        pltpu.make_async_copy(colors_hbm, colors_ref, sems.at[2]),
    ]
    for copy in copies:
        copy.start()
    even = is_even("gy")
    high, low = pl.multiple_of(by_parity(even, ny - TILE, 0), TILE), pl.multiple_of(by_parity(even, 0, ny - TILE), TILE)
    sent = []

    def send(begin, count):
        fields = pl.ds(begin, count)
        for target, source in (
            (first_hbm, own_ref.at[fields, :, pl.ds(high, TILE)]),
            (other_hbm, own_ref.at[fields, :, pl.ds(low, TILE)]),
            (own_hbm, own_ref.at[fields]),
        ):
            copy = pltpu.make_async_copy(source, target.at[fields], out_sems.at[len(sent)])
            copy.start()
            sent.append(copy)

    copies[1].wait()
    send(0, 3)
    copies[2].wait()
    own_ref[3:6] = colors_ref[...].astype(jnp.float32)
    copies[0].wait()

    def look_up(x, carry):
        label = labels_ref[x]
        value = jnp.zeros(label.shape, jnp.float32)
        for region in range(table_ref.shape[0]):
            value = jnp.where(label == region, table_ref[region], value)
        own_ref[6, x] = value
        return carry

    lax.fori_loop(0, nx, look_up, 0)
    send(3, 3)
    for copy in sent[:3]:
        copy.wait()
    send(6, 1)
    for copy in sent[3:]:
        copy.wait()


def side_kernel(sides, own_ref, *refs):
    nx, ny, nz = own_ref.shape[1:]
    *refs, low_ref, high_ref = refs
    low_ref[...] = own_ref[:, 0:HALO]
    high_ref[...] = own_ref[:, nx - HALO : nx]
    even, even_y = is_even("gz"), is_even("gy")
    group = lane_group((ny, nx * TILE))
    for side in range(sides):
        packed_ref, first_ref, other_ref = refs[side::sides]
        tail = even if side == 0 else jnp.logical_not(even)
        edge = pl.multiple_of(jnp.where(tail, nz - LANES, 0), LANES)
        turn = jnp.where(tail, TILE, 0)
        for field in range(NFIELD):
            packed = jnp.zeros((ny, nx * TILE), jnp.float32)
            for x in range(nx):
                row = own_ref[field, x, :, pl.ds(edge, LANES)]
                moved = pltpu.roll(row, (x * TILE) % LANES + turn, 1)
                if nx * TILE > LANES:
                    moved = jnp.tile(moved, (1, nx * TILE // LANES))
                packed = jnp.where(group == x, moved, packed)
            packed_ref[field] = packed
        for out_ref, tail_y in ((first_ref, even_y), (other_ref, jnp.logical_not(even_y))):
            edge = pl.multiple_of(jnp.where(tail_y, ny - TILE, 0), TILE)
            out_ref[...] = packed_ref[:, pl.ds(edge, TILE), :]


def third_kernel(sides, low_ref, high_ref, near_ref, far_ref, *refs):
    first_ref, other_ref = refs[3 * sides :]
    nx, ny = near_ref.shape[1], low_ref.shape[2]
    even_y = is_even("gy")
    below = pl.multiple_of(jnp.where(even_y, TILE + ny, 0), TILE)
    above = pl.multiple_of(jnp.where(even_y, 0, TILE + ny), TILE)
    even = is_even("gx")
    for out_ref, tail in ((first_ref, even), (other_ref, jnp.logical_not(even))):
        edge = jnp.where(tail, nx - HALO, 0)
        for end_ref, chosen in ((high_ref, tail), (low_ref, jnp.logical_not(tail))):

            @pl.when(chosen)
            def _(end_ref=end_ref, out_ref=out_ref):
                out_ref[:, 0:HALO, TILE : TILE + ny, :] = end_ref[...]

        out_ref[:, 0:HALO, pl.ds(below, TILE), :] = near_ref[:, pl.ds(edge, HALO)]
        out_ref[:, 0:HALO, pl.ds(above, TILE), :] = far_ref[:, pl.ds(edge, HALO)]
        for side in range(sides):
            side_ref, corner_ref, far_corner_ref = refs[side : 3 * sides : sides]
            out_ref[:, HALO + side, TILE : TILE + ny, :] = side_ref[...]
            out_ref[:, HALO + side, pl.ds(below, TILE), :] = corner_ref[...]
            out_ref[:, HALO + side, pl.ds(above, TILE), :] = far_corner_ref[...]


def by_parity(even, when_even, when_odd):
    return jnp.where(even, when_even, when_odd)


def neighbour_rows(ref, index, tile, shift, rows):
    if 0 <= tile + shift and tile + shift + TILE <= rows:
        return ref[index + (pl.ds(tile + shift, TILE),)]
    return pltpu.roll(ref[index + (pl.ds(tile, TILE),)], -shift % TILE, 0)


def over(first, count, body, choices=(4, 3, 5, 2)):
    unroll = min(choices, key=lambda u: (count % u) if u <= count else count)
    trips = count // unroll

    def step(trip, carry):
        for part in range(unroll):
            body(first + trip * unroll + part)
        return carry

    if trips > 1:
        lax.fori_loop(0, trips, step, 0)
    elif trips:
        step(0, 0)
    for part in range(trips * unroll, count):
        body(first + part)


class Window:
    def __init__(self, refs, table_ref):
        (self.cells, self.edges, self.edges_up, self.faces, self.faces_down, self.inverse,
         self.inside, self.conduct_down, self.weight, self.nodes, self.nodes_up,
         self.nodes_down, self.step_dir, self.rhs) = refs
        self.columns, self.rows = self.cells.shape[2:4]
        self.tiles = tuple(range(0, self.rows, TILE))
        self.own_tiles = self.tiles[1:-1]
        self.node_rows = self.nodes.shape[4]
        self.node_tiles = tuple(range(0, self.node_rows, TILE))
        self.own_columns = self.columns - 1
        self.lane = lax.broadcasted_iota(jnp.int32, (TILE, LANES), 1)
        top = table_ref[0]
        for region in range(1, table_ref.shape[0]):
            top = jnp.maximum(top, table_ref[region])
        upper = 13.0 * jnp.full((TILE, LANES), top, jnp.float32)
        lower = upper / 30.0
        centre = 0.5 * (upper + lower)
        half_width = 0.5 * (upper - lower)
        ratio = centre / half_width
        damping = 1.0 / ratio
        self.by_centre = 1.0 / centre
        self.terms = []
        for _ in range(1, NCHEB):
            damping_next = 1.0 / (2.0 * ratio - damping)
            self.terms.append((damping_next * damping, 2.0 * damping_next / half_width))
            damping = damping_next

    def up_z(self, values):
        moved = [pltpu.roll(v, LANES - 1, 1) for v in values]
        return [
            jnp.where(self.lane == LANES - 1, moved[(c + 1) % len(moved)], moved[c])
            for c in range(len(moved))
        ]

    def down_z(self, values):
        moved = [pltpu.roll(v, 1, 1) for v in values]
        return [jnp.where(self.lane == 0, moved[c - 1], moved[c]) for c in range(len(moved))]

    def spread(self, field, x, sources, group_at):
        even_z = is_even("gz")
        group = self.lane // TILE
        last_group = LANES // TILE - 1
        for tile in self.tiles:
            tail = jnp.zeros((TILE, LANES), jnp.float32)
            for side, source in enumerate(sources):
                upper = even_z if side == 0 else jnp.logical_not(even_z)
                at_lane = lax.rem(group_at * TILE, LANES)
                turn = LANES - at_lane + by_parity(upper, 0, LANES - TILE)
                moved = pltpu.roll(source(tile), lax.rem(turn, LANES), 1)
                tail = jnp.where(group == by_parity(upper, 0, last_group), moved, tail)
            self.cells[field, x, self.own_columns, pl.ds(tile, TILE)] = tail

    def prepare(self, x):
        for tile in self.tiles:
            here = pl.ds(tile, TILE)
            sigma, first = [], [[], []]
            for c in range(self.columns):
                value = self.cells[6, x, c, here]
                sigma.append(value)
                within = value > 0.0
                inv = jnp.where(within, 1.0 / (16.0 + value), 0.0)
                self.inverse[x, c, here] = inv
                self.inside[x, c, here] = jnp.where(within, 1.0, 0.0)
                for b in range(3):
                    start = jnp.where(
                        self.cells[3 + b, x, c, here] == 0.0, self.cells[b, x, c, here] * inv, 0.0
                    )
                    self.edges[0, b, x, c, here] = start
                    if b < 2:
                        first[b].append(start)
            for b in range(2):
                for c, value in enumerate(self.up_z(first[b])):
                    self.edges_up[0, b, x, c, here] = value
            for c, value in enumerate(self.down_z(sigma)):
                self.conduct_down[x, c, here] = value

    def curl(self, x, old, final):
        edges, edges_up = self.edges, self.edges_up
        for tile in self.tiles[:-1] if final else self.tiles:
            here = pl.ds(tile, TILE)
            turned = [[], []]
            for c in range(self.columns):
                keep = self.inside[x, c, here]
                ex, ey, ez = (edges[old, b, x, c, here] for b in range(3))
                ex_y = neighbour_rows(edges, (old, 0, x, c), tile, 1, self.rows)
                ez_y = neighbour_rows(edges, (old, 2, x, c), tile, 1, self.rows)
                face_x = (ey - edges_up[old, 1, x, c, here] + ez_y - ez) * keep
                face_y = (ez - edges[old, 2, x + 1, c, here] + edges_up[old, 0, x, c, here] - ex) * keep
                face_z = (ex - ex_y + edges[old, 1, x + 1, c, here] - ey) * keep
                for b, face in enumerate((face_x, face_y, face_z)):
                    self.faces[b, x, c, here] = face
                    if b < 2:
                        turned[b].append(face)
            for b in range(2):
                for c, value in enumerate(self.down_z(turned[b])):
                    self.faces_down[b, x, c, here] = value

    def update(self, x, old, color, final):
        faces, faces_down = self.faces, self.faces_down
        for tile in self.own_tiles if final else self.tiles:
            here = pl.ds(tile, TILE)
            turned = [[], []]
            for c in range(self.own_columns if final else self.columns):
                inv = self.inverse[x, c, here]
                fx, fy, fz = (faces[b, x, c, here] for b in range(3))
                fx_y = neighbour_rows(faces, (0, x, c), tile, -1, self.rows)
                fz_y = neighbour_rows(faces, (2, x, c), tile, -1, self.rows)
                back = (
                    (fz - fz_y) - (fy - faces_down[1, x, c, here]),
                    (fx - faces_down[0, x, c, here]) - (fz - faces[2, x - 1, c, here]),
                    (fy - faces[1, x - 1, c, here]) - (fx - fx_y),
                )
                for b in range(3):
                    own = self.edges[old, b, x, c, here]
                    fresh = (16.0 * own + (self.cells[b, x, c, here] - back[b])) * inv
                    fresh = jnp.where(self.cells[3 + b, x, c, here] == color, fresh, own)
                    self.edges[1 - old, b, x, c, here] = fresh
                    if b < 2:
                        turned[b].append(fresh)
            if not final:
                for b in range(2):
                    for c, value in enumerate(self.up_z(turned[b])):
                        self.edges_up[1 - old, b, x, c, here] = value

    def smooth(self, turn, first, count):
        old, color, final = (turn - 1) % 2, float(turn % NCOL), turn == HALO
        over(first - 1, count + 1, lambda x: self.curl(x, old, final), CURL_UNROLL)
        over(first, count, lambda x: self.update(x, old, color, final), (HALO,) if count == HALO else UPDATE_UNROLL)

    def start_nodal(self, x):
        cells = self.cells
        for tile in self.node_tiles:
            here, row = pl.ds(tile, TILE), tile + TILE - NCHEB
            at, under = pl.ds(row, TILE), pl.ds(row - 1, TILE)
            third_down = self.down_z([cells[2, x, c, at] for c in range(self.columns)])
            parts = [[] for _ in range(4)]
            for c in range(self.columns):
                keep = self.inside[x, c, at]
                pairs = (
                    (cells[0, x, c, at], cells[0, x - 1, c, at]),
                    (cells[1, x, c, at], cells[1, x, c, under]),
                    (cells[2, x, c, at], third_down[c]),
                )
                gap = (pairs[0][1] - pairs[0][0]) + (pairs[1][1] - pairs[1][0])
                gap = gap + (pairs[2][1] - pairs[2][0])
                values = [gap * keep] + [(0.5 * keep) * (a + b) for a, b in pairs]
                self.weight[x, c, here] = (
                    3.0 * cells[6, x, c, at] + cells[6, x - 1, c, at]
                    + cells[6, x, c, under]
                    + self.conduct_down[x, c, at]
                )
                for f, value in enumerate(values):
                    self.rhs[f, x, c, here] = value
                    value = value * self.by_centre
                    self.step_dir[f, x, c, here] = value
                    self.nodes[0, f, x, c, here] = value
                    parts[f].append(value)
            for f in range(4):
                for c, value in enumerate(self.up_z(parts[f])):
                    self.nodes_up[f, x, c, here] = value
                for c, value in enumerate(self.down_z(parts[f])):
                    self.nodes_down[f, x, c, here] = value

    def chebyshev(self, x, turn):
        old, final = (turn - 1) % 2, turn == NCHEB - 1
        keep_by, gain = self.terms[turn - 1]
        nodes, cells = self.nodes, self.cells
        for tile in self.node_tiles:
            here, row = pl.ds(tile, TILE), tile + TILE - NCHEB
            at, under = pl.ds(row, TILE), pl.ds(row - 1, TILE)
            parts = [[] for _ in range(4)]
            for c in range(self.columns):
                sigma, sigma_x = cells[6, x, c, at], cells[6, x - 1, c, at]
                sigma_y = cells[6, x, c, under]
                sigma_z = self.conduct_down[x, c, at]
                total, gained = self.weight[x, c, here], gain * self.inside[x, c, at]
                for f in range(4):
                    value = nodes[old, f, x, c, here]
                    above = nodes[old, f, x + 1, c, here] + self.nodes_up[f, x, c, here]
                    above = above + neighbour_rows(nodes, (old, f, x, c), tile, 1, self.node_rows)
                    below = neighbour_rows(nodes, (old, f, x, c), tile, -1, self.node_rows)
                    applied = (total if f == 0 else total + sigma) * value - sigma * above
                    applied = applied - sigma_x * nodes[old, f, x - 1, c, here]
                    applied = applied - sigma_y * below
                    applied = applied - sigma_z * self.nodes_down[f, x, c, here]
                    rest = self.rhs[f, x, c, here] - applied
                    moved = keep_by * self.step_dir[f, x, c, here] + gained * rest
                    value = value + moved
                    if not final:
                        self.step_dir[f, x, c, here] = moved
                    nodes[1 - old, f, x, c, here] = value
                    parts[f].append(value)
            for f in range(4):
                if not final or f in (0, 3):
                    for c, value in enumerate(self.up_z(parts[f])):
                        self.nodes_up[f, x, c, here] = value
                if not final:
                    for c, value in enumerate(self.down_z(parts[f])):
                        self.nodes_down[f, x, c, here] = value

    def nodal(self, first, count, shrink):
        over(first(0), count, self.start_nodal, START_UNROLL)
        for turn in range(1, NCHEB):
            over(first(turn), count - shrink * turn, lambda x: self.chebyshev(x, turn), NODAL_UNROLL)

    def correction(self, x, tile, c):
        done, nodes = (NCHEB - 1) % 2, self.nodes
        row = tile - TILE + NCHEB
        here = pl.ds(row, TILE)
        node = nodes[done, 0, x, c, here]
        ups = (
            (nodes[done, 0, x + 1, c, here], nodes[done, 1, x + 1, c, here]),
            tuple(nodes[done, f, x, c, pl.ds(row + 1, TILE)] for f in (0, 2)),
            (self.nodes_up[0, x, c, here], self.nodes_up[3, x, c, here]),
        )
        return [
            (node_up - node) + 0.5 * (nodes[done, 1 + b, x, c, here] + mean_up)
            for b, (node_up, mean_up) in enumerate(ups)
        ]

    def smoothed(self, x, tile, c):
        return [self.edges[HALO % 2, b, x, c, pl.ds(tile, TILE)] for b in range(3)]


def row_at(tile, c):
    return pl.ds(tile - TILE, TILE), pl.ds(c * LANES, LANES)


def inner_kernel(
    sides, own_hbm, near_hbm, far_hbm, met_hbm, mine_hbm, table_ref,
    part_ref, edges_ref, edges_up_ref, cells_ref, terms_ref, weight_ref, nodes_ref, shifted_ref, *rest,
):
    *arrays, packed, sems = rest
    window = Window(arrays, table_ref)
    cells = window.cells
    nx, ny, nz = part_ref.shape[1:]
    even_x, even_y = is_even("gx"), is_even("gy")
    below = pl.multiple_of(by_parity(even_y, TILE + ny, 0), TILE)
    above = pl.multiple_of(by_parity(even_y, 0, TILE + ny), TILE)
    own_at, met_at = by_parity(even_x, 0, HALO), by_parity(even_x, nx, 0)
    span = pl.ds(own_at, nx)
    copies = []
    if sides:
        copies += [
            (mine_hbm.at[:, pl.ds(HALO, sides)], packed.at[0]),
            (met_hbm.at[:, pl.ds(HALO, sides)], packed.at[1]),
        ]
    early = len(copies)
    for c in range(window.own_columns):
        z = pl.ds(c * LANES, LANES)
        copies += [
            (own_hbm.at[:, :, :, z], cells.at[:, span, c, pl.ds(TILE, ny)]),
            (near_hbm.at[:, :, :, z], cells.at[:, span, c, pl.ds(below, TILE)]),
            (far_hbm.at[:, :, :, z], cells.at[:, span, c, pl.ds(above, TILE)]),
            (met_hbm.at[:, pl.ds(0, HALO), :, z], cells.at[:, pl.ds(met_at, HALO), c]),
        ]
    copies = [pltpu.make_async_copy(src, dst, sems.at[n]) for n, (src, dst) in enumerate(copies)]
    for copy in copies:
        copy.start()
    for copy in copies[:early]:
        copy.wait()

    met_group = by_parity(even_x, 0, nx - HALO)

    def sources(place, field, group):
        column = group * TILE // LANES if isinstance(group, int) else 0
        return [
            lambda tile, side=side: packed[
                place, field, side, pl.ds(tile, TILE), pl.ds(column * LANES, LANES)
            ]
            for side in range(sides)
        ]

    def spread(field, carry):
        for x in range(nx):
            window.spread(field, own_at + x, sources(0, field, x), x)
        for x in range(HALO):
            window.spread(field, met_at + x, sources(1, field, met_group), met_group + x)
        return carry

    lax.fori_loop(0, NFIELD, spread, 0)
    for copy in copies[early:]:
        copy.wait()
    size = nx + HALO
    over(0, size, window.prepare, PREPARE_UNROLL)
    for turn in range(1, HALO + 1):
        window.smooth(turn, turn, size - 2 * turn)
    reach = NCHEB - 1
    count = nx + reach
    nodal_at = by_parity(even_x, 1, NCHEB)
    window.nodal(lambda turn: nodal_at + turn, count, 2)

    both, both_at = nx - HALO, by_parity(even_x, HALO, 0)
    alone, alone_at = HALO - NCHEB, by_parity(even_x, NCHEB, nx - HALO)

    def result(x, smoothed):
        for tile in window.own_tiles:
            for c in range(window.own_columns):
                values = window.correction(own_at + x, tile, c)
                if smoothed:
                    values = [a + b for a, b in zip(window.smoothed(own_at + x, tile, c), values)]
                for b, value in enumerate(values):
                    part_ref[(b, x) + row_at(tile, c)] = value

    over(both_at, both, lambda x: result(x, True))
    over(alone_at, alone, lambda x: result(x, False))

    edge_at = by_parity(even_x, 0, size - HALO - 1)
    edges_ref[...] = window.edges[:, :, pl.ds(edge_at, HALO + 1)]
    edges_up_ref[...] = window.edges_up[:, :, pl.ds(edge_at, HALO + 1)]
    cells_ref[...] = cells[:, pl.ds(edge_at, HALO + 1)]
    terms_ref[0] = window.inverse[pl.ds(edge_at, HALO + 1)]
    terms_ref[1] = window.inside[pl.ds(edge_at, HALO + 1)]
    terms_ref[2] = window.conduct_down[pl.ds(edge_at, HALO + 1)]
    node_at = by_parity(even_x, 1, size - NCHEB)
    weight_ref[...] = window.weight[pl.ds(node_at, NCHEB)]
    nodes_ref[...] = window.nodes[:, :, pl.ds(node_at, NCHEB)]
    for n, ref in enumerate((window.nodes_up, window.nodes_down, window.step_dir, window.rhs)):
        shifted_ref[n] = ref[:, pl.ds(node_at, NCHEB)]


def outer_kernel(
    sides, met_ref, part_ref, edges_ref, edges_up_ref, cells_ref, terms_ref, weight_ref,
    nodes_ref, shifted_ref, table_ref, out_ref, *arrays,
):
    window = Window(arrays, table_ref)
    cells = window.cells
    nx = out_ref.shape[1]
    even_x = is_even("gx")
    size = 2 * HALO + 2
    met_at = by_parity(even_x, 0, size - HALO)
    edge_at = by_parity(even_x, HALO, 1)
    window.edges[:, :, pl.ds(edge_at, HALO + 1)] = edges_ref[...]
    window.edges_up[:, :, pl.ds(edge_at, HALO + 1)] = edges_up_ref[...]
    cells[:, pl.ds(edge_at, HALO + 1)] = cells_ref[...]
    window.inverse[pl.ds(edge_at, HALO + 1)] = terms_ref[0]
    window.inside[pl.ds(edge_at, HALO + 1)] = terms_ref[1]
    window.conduct_down[pl.ds(edge_at, HALO + 1)] = terms_ref[2]
    node_at = by_parity(even_x, HALO + 1, HALO + 2 - NCHEB)
    window.weight[pl.ds(node_at, NCHEB)] = weight_ref[...]
    window.nodes[:, :, pl.ds(node_at, NCHEB)] = nodes_ref[...]
    for n, ref in enumerate((window.nodes_up, window.nodes_down, window.step_dir, window.rhs)):
        ref[:, pl.ds(node_at, NCHEB)] = shifted_ref[n]
    for c in range(window.own_columns):
        cells[:, pl.ds(met_at, HALO), c] = met_ref[:, 0:HALO, :, c * LANES : (c + 1) * LANES]
    met_group = by_parity(even_x, nx - HALO, 0)

    def spread(field, carry):
        sources = [
            lambda tile, side=side: met_ref[field, HALO + side, pl.ds(tile, TILE), 0:LANES]
            for side in range(sides)
        ]
        for x in range(HALO):
            window.spread(field, met_at + x, sources, met_group + x)
        return carry

    lax.fori_loop(0, NFIELD, spread, 0)
    over(met_at, HALO, window.prepare, (HALO,))
    for turn in range(1, HALO + 1):
        window.smooth(turn, by_parity(even_x, turn, HALO + 2 - turn), HALO)
    start = by_parity(even_x, HALO + 1 - NCHEB, HALO + 2)
    window.nodal(lambda turn: by_parity(even_x, start + turn, start - turn), NCHEB, 0)

    own_at = by_parity(even_x, HALO, 2 + HALO - nx)
    both, both_at = nx - HALO, by_parity(even_x, HALO, 0)
    alone, alone_at = HALO - NCHEB, by_parity(even_x, NCHEB, nx - HALO)
    rest_at = by_parity(even_x, 0, nx - NCHEB)
    out_ref[:, pl.ds(both_at, both)] = part_ref[:, pl.ds(both_at, both)]

    def result(x, corrected):
        for tile in window.own_tiles:
            for c in range(window.own_columns):
                at = row_at(tile, c)
                if corrected:
                    values = [part_ref[(b, x) + at] for b in range(3)]
                else:
                    values = window.correction(own_at + x, tile, c)
                for b, value in enumerate(window.smoothed(own_at + x, tile, c)):
                    out_ref[(b, x) + at] = value + values[b]

    over(alone_at, alone, lambda x: result(x, True))
    over(rest_at, NCHEB, lambda x: result(x, False))


def on_device(right_side, labels, colors, table):
    nx, ny, nz = labels.shape
    sides = sum(1 for pairs in swaps_of(lax.axis_size("gz")) if pairs)
    vmem, smem = pl.BlockSpec(memory_space=pltpu.VMEM), pl.BlockSpec(memory_space=pltpu.SMEM)
    anywhere = pl.BlockSpec(memory_space=pl.ANY)

    def array(*shape):
        return jax.ShapeDtypeStruct(shape, jnp.float32)

    def call(kernel, name, outs, in_specs, scratch=(), limit=12, flops=0, out=vmem):
        return pl.pallas_call(
            lambda *refs: kernel(sides, *refs),
            out_shape=outs,
            in_specs=in_specs,
            out_specs=jax.tree.map(lambda _: out, outs),
            scratch_shapes=scratch,
            compiler_params=pltpu.CompilerParams(vmem_limit_bytes=limit << 20),
            cost_estimate=pl.CostEstimate(flops=flops, bytes_accessed=1 << 20, transcendentals=0),
            name=name,
        )

    hbm = pl.BlockSpec(memory_space=pltpu.HBM)
    own, *second = call(
        start_kernel, "start", [array(NFIELD, nx, ny, nz)] + [array(NFIELD, nx, TILE, nz)] * 2,
        [hbm, hbm, hbm, smem],
        [
            pltpu.VMEM((nx, ny, nz), jnp.int32), pltpu.VMEM((3, nx, ny, nz), jnp.int32),
            pltpu.VMEM((NFIELD, nx, ny, nz), jnp.float32),
            pltpu.SemaphoreType.DMA((3,)), pltpu.SemaphoreType.DMA((9,)),
        ],
        limit=START_LIMIT, out=hbm,
    )(right_side, labels, colors, table)
    along_y, along_z = swaps_of(lax.axis_size("gy")), swaps_of(lax.axis_size("gz"))[:sides]
    near = exchange(second[0], "gy", along_y[0])
    far = exchange(second[1], "gy", along_y[1])
    *thirds, low, high = call(
        side_kernel, "pack_third",
        [array(NFIELD, ny, nx * TILE)] * sides + [array(NFIELD, TILE, nx * TILE)] * (2 * sides)
        + [array(NFIELD, HALO, ny, nz)] * 2,
        [vmem],
    )(own)
    corners = [
        exchange(message, ("gy", "gz"), joint_pairs(pairs, across, lax.axis_size("gz")))
        for message, (pairs, across) in zip(
            thirds[sides:], [(pairs, across) for pairs in along_y for across in along_z]
        )
    ]
    thirds = [exchange(message, "gz", pairs) for message, pairs in zip(thirds, along_z)]
    rows = ny + 2 * TILE
    first = call(
        third_kernel, "pack_first", [array(NFIELD, HALO + sides, rows, nz)] * 2,
        [vmem] * (4 + 3 * sides), limit=14,
    )(low, high, near, far, *thirds, *corners)
    along_x = swaps_of(lax.axis_size("gx"))
    met = exchange(first[0], "gx", along_x[0])
    late = exchange(first[1], "gx", along_x[1])
    columns = nz // LANES + 1

    node_rows = ny + 2 * NCHEB

    def slices(*lead, depth, rows=rows):
        return (*lead, depth, columns, rows, LANES)

    def arrays(depth):
        shapes = [(lead, rows) for lead in ((NFIELD,), (2, 3), (2, 2), (3,), (2,), (), (), ())]
        shapes += [(lead, node_rows) for lead in ((), (2, 4), (4,), (4,), (4,), (4,))]
        return [
            pltpu.VMEM(slices(*lead, depth=depth, rows=rows), jnp.float32) for lead, rows in shapes
        ]

    edge, node = HALO + 1, NCHEB
    state = call(
        inner_kernel, "solve_inner",
        [
            array(3, nx, ny, nz), array(*slices(2, 3, depth=edge)),
            array(*slices(2, 2, depth=edge)), array(*slices(NFIELD, depth=edge)),
            array(*slices(3, depth=edge)), array(*slices(depth=node, rows=node_rows)),
            array(*slices(2, 4, depth=node, rows=node_rows)),
            array(*slices(4, 4, depth=node, rows=node_rows)),
        ],
        [anywhere] * 5 + [smem],
        arrays(nx + HALO) + [
            pltpu.VMEM((2, NFIELD, max(sides, 1), rows, nx * TILE), jnp.float32),
            pltpu.SemaphoreType.DMA((4 * (columns - 1) + 2,)),
        ],
        limit=40, flops=1 << 34,
    )(own, near, far, met, first[0], table)
    return call(
        outer_kernel, "solve_outer", array(3, nx, ny, nz), [vmem] * 9 + [smem],
        arrays(2 * HALO + 2), limit=30,
    )(late, *state, table)


def solution(mesh):
    in_specs = (P(None, "gx", "gy", "gz"), P("gx", "gy", "gz"), P(None, "gx", "gy", "gz"), P())
    out_specs = P(None, "gx", "gy", "gz")
    return jax.shard_map(
        on_device, mesh=mesh, in_specs=in_specs, out_specs=out_specs, check_vma=False
    )
```
